768 devices in a mesh: group: 192 (over y, z, core), peer: 4 (over x).
Axes of the slice: x: 4, y: 8, z: 12, core: 2. Of those that a mesh axis runs over, the one named last changes fastest.
Arguments:
- queries: bfloat16 [98304, 1024], P(('group', 'peer')), may hold values from -40 to 40
- keys_values: bfloat16 [98304, 256], P(('group', 'peer')), may hold values from -40 to 40
- doc_lengths: int32 [25], replicated, may hold values from 1 to 4096, 98304 in all
Outputs:
- attended: bfloat16 [98304, 1024], P(('group', 'peer'))
- log_total: float32 [98304, 8], P(('group', 'peer'))
The draws below stay inside these ranges and needn't reach their ends.
Inputs may be any that keep to these rules, and one draw needn't show every extreme that they name: `doc_lengths`: every document has 1 to 4096 tokens, the lengths sum to 98304, and one document has exactly 4096.
All inputs are finite; a program needn't handle non-finite values.
Results may differ from the reference program's by a relative error of at most 0.005.
Values may be sent and summed in bfloat16 or wider, within the bound.
No kernel may reach another device: no remote copies, remote signals or barrier semaphores. Data moves between devices by JAX's collectives and lax.ppermute only.
A program may use at most 32 MiB of HBM per device.

```python
import math
import jax
import jax.numpy as jnp
import numpy as np
from jax import lax

H = 8
HD = 128
TOK_DEV = 128
SPAN = 32
TOKENS = 98304
LMAX = 4096
NDOCS = 25


def draw_queries(key, part):
    base = jnp.clip(jax.random.normal(jax.random.fold_in(key, 21), (TOKENS, H * HD), jnp.float32), -6.0, 6.0)
    return base.astype(jnp.bfloat16)


def draw_keys_values(key, part):
    keys_part = jnp.clip(jax.random.normal(jax.random.fold_in(key, 31), (TOKENS, HD), jnp.float32), -6.0, 6.0)
    values_part = jnp.clip(jax.random.normal(jax.random.fold_in(key, 32), (TOKENS, HD), jnp.float32), -6.0, 6.0)
    return jnp.concatenate([keys_part, values_part], axis=1).astype(jnp.bfloat16)


def length_profile(count, total, reach, lean):
    loads = [(1 << 20) // math.isqrt(rank ** lean) + 1 for rank in range(2, count + 1)]
    surplus, counts = total - reach - (count - 1), [1] * (count - 1)
    while surplus > 0:
        free = [i for i in range(count - 1) if counts[i] < reach]
        mass, remaining = sum([loads[i] for i in free]), surplus
        for i in free:
            more = min(reach - counts[i], max(1, remaining * loads[i] // mass), surplus)
            counts[i] = counts[i] + more
            surplus = surplus - more
    return np.array([reach] + counts)


def ragged(rng, amount, total, most, slope):
    if amount == 2:
        one = jax.random.randint(rng, (), max(1, total - most), min(most, total - 1) + 1)
        return jnp.stack([one, total - one])
    lengths = jnp.asarray(length_profile(amount, total, most, slope), jnp.int32)
    couples = (amount - 1) // 2
    donor, taker = lengths[1:1 + 2 * couples:2], lengths[2:2 + 2 * couples:2]
    margin = jnp.minimum(donor - 1, most - taker)
    passed = jax.random.randint(jax.random.fold_in(rng, 1), (couples,), 0, 1 << 20) % (margin + 1)
    lengths = lengths.at[1:1 + 2 * couples:2].set(donor - passed).at[2:2 + 2 * couples:2].set(taker + passed)
    return lengths[jax.random.permutation(jax.random.fold_in(rng, 2), amount)]


def setup_inputs(seed: int = 0) -> dict:
    seeds = jax.random.split(jax.random.key(seed), 4)
    return {
        "queries": draw_queries(jax.random.fold_in(seeds[3], 71), 0),
        "keys_values": draw_keys_values(jax.random.fold_in(seeds[3], 71), 0),
        "doc_lengths": ragged(seeds[2], NDOCS, TOKENS, LMAX, 2).astype(jnp.int32),
    }


def doc_index(positions, doc_ends):
    return lax.optimization_barrier(jnp.sum((positions[:, None] >= doc_ends[None, :]).astype(jnp.int32), axis=1)).astype(jnp.int32)

def reference(queries, keys_values, doc_lengths):
    doc_ends = jnp.cumsum(doc_lengths).astype(jnp.int32)
    lead_rows = SPAN * TOK_DEV
    padded = jnp.concatenate([jnp.zeros((lead_rows, 2 * HD), keys_values.dtype), keys_values], axis=0)
    score_scale = 1.0 / math.sqrt(HD)

    def per_block(block_number):
        row_start = (block_number * TOK_DEV).astype(jnp.int32)
        query_block = lax.dynamic_slice_in_dim(queries, row_start, TOK_DEV, 0).reshape(TOK_DEV, H, HD).astype(jnp.float32)
        kv_block = lax.dynamic_slice_in_dim(padded, row_start, lead_rows + TOK_DEV, 0).astype(jnp.float32)
        query_pos = row_start + jnp.arange(TOK_DEV, dtype=jnp.int32)
        key_pos = row_start - lead_rows + jnp.arange(lead_rows + TOK_DEV, dtype=jnp.int32)
        query_doc = doc_index(query_pos, doc_ends)
        key_doc = doc_index(key_pos, doc_ends)
        visible = (key_pos >= 0)[None, :] & (key_doc[None, :] == query_doc[:, None]) & (key_pos[None, :] <= query_pos[:, None])
        scores = jnp.einsum('thd,sd->ths', query_block, kv_block[:, :HD]) * score_scale
        scores = jnp.where(visible[:, None, :], scores, jnp.float32(-1e+30))
        rowmax = lax.optimization_barrier(jnp.max(scores, axis=-1))
        expon = jnp.exp(scores - rowmax[..., None])
        totals = lax.optimization_barrier(jnp.sum(expon, axis=-1))
        weights = expon.astype(jnp.bfloat16).astype(jnp.float32)
        summed = jnp.einsum('ths,sd->thd', weights, kv_block[:, HD:]) / totals[..., None]
        return (summed.reshape(TOK_DEV, H * HD).astype(jnp.bfloat16), rowmax + jnp.log(totals))
    attended, log_total = lax.map(per_block, jnp.arange(TOKENS // TOK_DEV, dtype=jnp.int32))
    return (attended.reshape(TOKENS, H * HD), log_total.reshape(TOKENS, H))
```

```python
import functools
import math

import jax
import jax.numpy as jnp
from jax import lax
from jax.experimental import pallas as pl
from jax.experimental.pallas import tpu as pltpu
from jax.sharding import PartitionSpec as P

ROWS = 128
HEADS = 8
WIDTH = 128
NEG = -1e30
LOG2E = math.log2(math.e)
F32 = jnp.float32


def attend_body(first, last, layout, sizes, own_group, own_peer, doc_ref, q_ref, *refs):
    n_kv = len(sizes)
    kv_refs = refs[:n_kv]
    refs = refs[n_kv:]
    if first:
        refs_in = None
    else:
        refs_in, refs = refs[:2], refs[2:]
    out_a, out_b, stat, acc = refs

    group = own_group()
    peer = own_peer()
    q_first = (group * 4 + peer) * ROWS

    def starts_at(pos):
        def step(d, carry):
            end, start = carry
            end = end + doc_ref[d]
            return end, jnp.where(end <= pos, end, start)

        return lax.fori_loop(0, doc_ref.shape[0], step, (jnp.int32(0), jnp.zeros_like(pos)), unroll=True)[1]

    start_low = starts_at(q_first)
    start_high = starts_at(q_first + ROWS - 1)
    row_pos = q_first + lax.broadcasted_iota(jnp.int32, (ROWS, 1), 0)
    row_start = starts_at(row_pos)

    lane = lax.broadcasted_iota(jnp.int32, (ROWS, WIDTH), 1)
    if first:
        stat[...] = jnp.where(lane < HEADS, F32(NEG), F32(0))
        acc[...] = jnp.zeros_like(acc)
    else:
        stat[...] = refs_in[0][...]
        acc[...] = refs_in[1][...]

    def process(tile, base, masked):
        keys = tile[:, :WIDTH]
        values = jnp.concatenate([tile[:, WIDTH:], jnp.ones((tile.shape[0], WIDTH), jnp.bfloat16)], axis=1)
        if masked:
            key_pos = base + lax.broadcasted_iota(jnp.int32, (ROWS, tile.shape[0]), 1)
            seen = (key_pos >= row_start) & (key_pos <= row_pos)
        stats = stat[...]
        new_stats = stats
        for h in range(HEADS):
            cols = slice(h * WIDTH, (h + 1) * WIDTH)
            score = lax.dot_general(
                q_ref[:, cols], keys, (((1,), (1,)), ((), ())), preferred_element_type=F32
            ) * F32(LOG2E / math.sqrt(WIDTH))
            if masked:
                score = jnp.where(seen, score, F32(NEG))
            old = stats[:, h : h + 1]
            new = jnp.maximum(old, jnp.max(score, axis=1, keepdims=True))
            weight = jnp.exp2(score - new).astype(jnp.bfloat16)
            fade = jnp.exp2(old - new)
            out = lax.dot_general(weight, values, (((1,), (0,)), ((), ())), preferred_element_type=F32)
            acc[:, cols] = acc[:, cols] * fade + out[:, :WIDTH]
            total = stats[:, HEADS + h : HEADS + h + 1] * fade + out[:, WIDTH : WIDTH + 1]
            new_stats = jnp.where(lane == h, new, jnp.where(lane == HEADS + h, total, new_stats))
        stat[...] = new_stats

    for kv_ref, count, place in zip(kv_refs, sizes, layout):
        def body(i, _, kv_ref=kv_ref, place=place):
            load, tile_group = place(kv_ref, i, group)
            base = tile_group * 4 * ROWS
            span = 4 * ROWS
            needed = (base + span > start_low) & (base < q_first + ROWS) & (base >= 0)
            whole = (base >= start_high) & (base + span <= q_first)

            @pl.when(needed & whole)
            def _():
                process(load(), base, False)

            @pl.when(needed & jnp.logical_not(whole))
            def _():
                process(load(), base, True)

            return 0

        lax.fori_loop(0, count, body, 0)

    if last:
        stats = stat[...]
        for h in range(HEADS):
            cols = slice(h * WIDTH, (h + 1) * WIDTH)
            out_a[:, cols] = (acc[:, cols] / stats[:, HEADS + h : HEADS + h + 1]).astype(out_a.dtype)
        logs = stats[:, :HEADS] * F32(math.log(2.0)) + jnp.log(stats[:, HEADS : 2 * HEADS])
        out_b[...] = logs
    else:
        out_a[...] = stat[...]
        out_b[...] = acc[...]


AXES = ("group", "peer")
TILE = 4 * ROWS


def attend(doc_lengths, queries, pieces, state, last):
    def place(other, back):
        def at(kv_ref, i, group):
            def load():
                return kv_ref[:, pl.ds(pl.multiple_of(i * ROWS, ROWS), ROWS), :].reshape(TILE, 2 * WIDTH)

            line, core = group // 2, group % 2
            return load, 2 * (line - back - i) + (1 - core if other else core)

        return at

    sizes = [kv.shape[1] // ROWS for kv, _, _ in pieces]
    layout = [place(other, back) for _, other, back in pieces]
    body = functools.partial(
        attend_body,
        state is None,
        last,
        layout,
        sizes,
        lambda: lax.axis_index("group"),
        lambda: lax.axis_index("peer"),
    )
    vmem = pl.BlockSpec(memory_space=pltpu.VMEM)
    operands = [doc_lengths, queries, *(kv for kv, _, _ in pieces), *(state or ())]
    if last:
        out_shape = (
            jax.ShapeDtypeStruct((ROWS, HEADS * WIDTH), jnp.bfloat16),
            jax.ShapeDtypeStruct((ROWS, HEADS), F32),
        )
    else:
        out_shape = (
            jax.ShapeDtypeStruct((ROWS, WIDTH), F32),
            jax.ShapeDtypeStruct((ROWS, HEADS * WIDTH), F32),
        )
    return pl.pallas_call(
        body,
        out_shape=out_shape,
        in_specs=[pl.BlockSpec(memory_space=pltpu.SMEM)] + [vmem] * (len(operands) - 1),
        out_specs=(vmem, vmem),
        scratch_shapes=[pltpu.VMEM((ROWS, WIDTH), F32), pltpu.VMEM((ROWS, HEADS * WIDTH), F32)],
    )(*operands)


def moved(value, source):
    count = lax.axis_size("group") * lax.axis_size("peer")
    pairs = [(source(t), t) for t in range(count) if source(t) >= 0]
    return lax.ppermute(value, AXES, pairs)


def shards(queries, keys_values, doc_lengths):
    column = [keys_values] + [moved(keys_values, lambda t, k=k: t - 8 * k) for k in (1, 2, 3, 4)]
    column = jnp.concatenate(column, axis=0)
    mine = lax.all_to_all(jnp.broadcast_to(column, (4, *column.shape)), "peer", 0, 0)
    other = moved(mine, lambda t: t ^ 4)
    state = attend(doc_lengths, queries, [(mine, False, 0)], None, False)
    return attend(doc_lengths, queries, [(other, True, 0)], state, True)


def solution(mesh):
    placed = (P(AXES, None), P(AXES, None), P())
    return jax.shard_map(
        shards,
        mesh=mesh,
        in_specs=placed,
        out_specs=(P(AXES, None), P(AXES, None)),
        check_vma=False,
    )
```

```python
import functools
import math

import jax
import jax.numpy as jnp
from jax import lax
from jax.experimental import pallas as pl
from jax.experimental.pallas import tpu as pltpu
from jax.sharding import PartitionSpec as P

ROWS = 128
HEADS = 8
WIDTH = 128
BLOCKS = 4
NEG = -1e30
LIMIT = 2.0**40
SCALE = math.log2(math.e) / math.sqrt(WIDTH)
F32 = jnp.float32
BF16 = jnp.bfloat16


def attend_body(first, last, places, own, doc_ref, q_ref, *refs):
    kv_refs, refs = refs[: len(places)], refs[len(places) :]
    if not first:
        stat_in, acc_in, refs = refs[0], refs[1], refs[2:]
    if last:
        out, log_out, stat, acc, bias = refs
    else:
        stat, acc, bias = refs
    group, peer = own()
    q_first = (group * 4 + peer) * ROWS

    def starts_at(pos):
        def step(d, carry):
            end, start = carry
            end = end + doc_ref[d]
            return end, jnp.where(end <= pos, end, start)

        return lax.fori_loop(0, doc_ref.shape[0], step, (jnp.int32(0), jnp.zeros_like(pos)), unroll=True)[1]

    start_low = starts_at(q_first)
    start_high = starts_at(q_first + ROWS - 1)
    row_pos = q_first + lax.broadcasted_iota(jnp.int32, (8, ROWS), 1)
    row_start = starts_at(row_pos)[:1]
    row_pos = row_pos[:1]
    query = [q_ref[:, h * WIDTH : (h + 1) * WIDTH].T for h in range(HEADS)]
    query = [jnp.concatenate(query[h : h + 2], axis=1) for h in range(0, HEADS, 2)]
    span = BLOCKS * ROWS

    def pair_rows(values, h):
        return jnp.concatenate([values[h : h + 1], values[h + 1 : h + 2]], axis=1)

    def operands(tile):
        values = jnp.concatenate([tile[:, WIDTH:].T, jnp.ones((16, span), BF16)], axis=0)
        return tile[:, :WIDTH], values

    def set_bias(base):
        key_pos = base + lax.broadcasted_iota(jnp.int32, (span, ROWS), 0)
        hidden = jnp.where((key_pos >= row_start) & (key_pos <= row_pos), F32(0), F32(NEG))
        bias[:, :ROWS] = hidden
        bias[:, ROWS:] = hidden

    def exact(tile, base):
        keys, values = operands(tile)
        set_bias(base)

        for p in range(HEADS // 2):
            h = 2 * p
            score = jnp.dot(keys, query[p], preferred_element_type=F32) * F32(SCALE) + bias[...]
            old = pair_rows(stat, h)
            new = jnp.maximum(old, jnp.max(score, axis=0, keepdims=True))
            fade = jnp.exp2(old - new)
            part = jnp.dot(values, jnp.exp2(score - new).astype(BF16), preferred_element_type=F32)
            for k in range(2):
                rows, cols = slice((h + k) * WIDTH, (h + k + 1) * WIDTH), slice(k * ROWS, (k + 1) * ROWS)
                acc[rows] = acc[rows] * fade[:, cols] + part[:WIDTH, cols]
                at = HEADS + h + k
                stat[at : at + 1] = stat[at : at + 1] * fade[:, cols] + part[WIDTH : WIDTH + 1, cols]
                stat[h + k : h + k + 1] = new[:, cols]

    def quick(tile, base, masked):
        keys, values = operands(tile)
        if masked:
            set_bias(base)
        for p in range(HEADS // 2):
            h = 2 * p
            held = pair_rows(stat, h)
            score = jnp.dot(keys, query[p], preferred_element_type=F32) * F32(SCALE) - held
            if masked:
                score = score + bias[...]
            part = jnp.dot(values, jnp.exp2(score).astype(BF16), preferred_element_type=F32)
            for k in range(2):
                rows, cols = slice((h + k) * WIDTH, (h + k + 1) * WIDTH), slice(k * ROWS, (k + 1) * ROWS)
                acc[rows] += part[:WIDTH, cols]
                at = HEADS + h + k
                stat[at : at + 1] += part[WIDTH : WIDTH + 1, cols]

    def run(fast):
        if first:
            stat[:HEADS] = jnp.full((HEADS, ROWS), NEG, F32)
            stat[HEADS:] = jnp.zeros((HEADS, ROWS), F32)
            acc[...] = jnp.zeros_like(acc)
        else:
            stat[...] = stat_in[...]
            acc[...] = acc_in[...]

        for n, (kv_ref, (slots, place)) in enumerate(zip(kv_refs, places)):

            def body(i, _, kv_ref=kv_ref, place=place, own_tile=first and n == 0):
                load, tile_group = place(kv_ref, i, group)
                base = tile_group * span
                needed = (base + span > start_low) & (base < q_first + ROWS) & (base >= 0)
                whole = (base >= start_high) & (base + span <= q_first)
                if not fast:

                    @pl.when(needed)
                    def _():
                        exact(load(), base)

                    return 0

                @pl.when(needed & whole)
                def _():
                    quick(load(), base, False)

                @pl.when(needed & jnp.logical_not(whole))
                def _():
                    quick(load(), base, True)

                return 0

            start = 0
            if fast and first and n == 0:
                load, tile_group = place(kv_ref, 0, group)
                exact(load(), tile_group * span)
                start = 1
            lax.fori_loop(start, slots, body, 0)

    run(True)

    @pl.when(jnp.logical_not(jnp.max(stat[HEADS:]) <= F32(LIMIT)))
    def _():
        run(False)

    if last:
        stats = stat[...]
        for h in range(HEADS):
            rows = slice(h * WIDTH, (h + 1) * WIDTH)
            out[:, rows] = (acc[rows] / stats[HEADS + h : HEADS + h + 1]).T.astype(BF16)
        log_out[...] = stats[:HEADS] * F32(math.log(2.0)) + jnp.log(stats[HEADS:])


def attend(doc_lengths, queries, pieces, state, last, own):
    places = [(kv.shape[1] // ROWS, place) for kv, place in pieces]
    vmem = pl.BlockSpec(memory_space=pltpu.VMEM)
    resident = [pltpu.with_memory_space_constraint(a, pltpu.VMEM) for a in (*(kv for kv, _ in pieces), *(state or ()))]
    operands = [doc_lengths, queries, *resident]
    state_shape = [(2 * HEADS, ROWS), (HEADS * WIDTH, ROWS)]
    bias = pltpu.VMEM((BLOCKS * ROWS, 2 * ROWS), F32)
    if last:
        out_shape = (
            jax.ShapeDtypeStruct((ROWS, HEADS * WIDTH), BF16),
            jax.ShapeDtypeStruct((HEADS, ROWS), F32),
        )
        scratch = [pltpu.VMEM(s, F32) for s in state_shape] + [bias]
    else:
        out_shape = tuple(pltpu.VMEM(s, F32) for s in state_shape)
        scratch = [bias]
    return pl.pallas_call(
        functools.partial(attend_body, state is None, last, places, own),
        out_shape=out_shape,
        in_specs=[pl.BlockSpec(memory_space=pltpu.SMEM)] + [vmem] * (len(operands) - 1),
        out_specs=(vmem, vmem),
        scratch_shapes=scratch,
        compiler_params=pltpu.CompilerParams(vmem_limit_bytes=16 << 20),
    )(*operands)


AXES = ("group", "peer")


def place(other, back):
    def at(kv_ref, i, group):
        def load():
            return kv_ref[:, pl.ds(pl.multiple_of(i * ROWS, ROWS), ROWS), :].reshape(BLOCKS * ROWS, 2 * WIDTH)

        line, core = group // 2, group % 2
        return load, 2 * (line - back - i) + (1 - core if other else core)

    return at


def own():
    return lax.axis_index("group"), lax.axis_index("peer")


def moved(value, source):
    count = lax.axis_size("group") * lax.axis_size("peer")
    pairs = [(source(t), t) for t in range(count) if source(t) >= 0]
    return lax.ppermute(value, AXES, pairs)


def shards(queries, keys_values, doc_lengths):
    column = [keys_values] + [moved(keys_values, lambda t, k=k: t - 8 * k) for k in (1, 2, 3, 4)]
    column = jnp.concatenate(column, axis=0)
    mine = lax.all_to_all(jnp.broadcast_to(column, (4, *column.shape)), "peer", 0, 0)
    other = moved(mine, lambda t: t ^ 4)
    state = attend(doc_lengths, queries, [(mine, place(False, 0))], None, False, own)
    attended, log_total = attend(doc_lengths, queries, [(other, place(True, 0))], state, True, own)
    return attended, log_total.T


def solution(mesh):
    placed = (P(AXES, None), P(AXES, None), P())
    return jax.shard_map(
        shards,
        mesh=mesh,
        in_specs=placed,
        out_specs=(P(AXES, None), P(AXES, None)),
        check_vma=False,
    )
```

```python
import functools
import math

import jax
import jax.numpy as jnp
from jax import lax
from jax.experimental import pallas as pl
from jax.experimental.pallas import tpu as pltpu
from jax.sharding import PartitionSpec as P


ROWS = 128
HEADS = 8
WIDTH = 128
BLOCKS = 4
NEG = -1e30
LIMIT = 2.0**40
SCALE = math.log2(math.e) / math.sqrt(WIDTH)
F32 = jnp.float32
BF16 = jnp.bfloat16


def starts_at(doc_ref, pos):
    def step(d, carry):
        end, start = carry
        end = end + doc_ref[d]
        return end, jnp.where(end <= pos, end, start)

    return lax.fori_loop(0, doc_ref.shape[0], step, (jnp.int32(0), jnp.zeros_like(pos)), unroll=True)[1]


def prepare_body(own, doc_ref, q_ref, query, row_start):
    for h in range(HEADS):
        rows = slice(h // 2 * WIDTH, (h // 2 + 1) * WIDTH)
        query[rows, h % 2 * ROWS : (h % 2 + 1) * ROWS] = q_ref[:, h * WIDTH : (h + 1) * WIDTH].T
    group, peer = own()
    row_pos = (group * 4 + peer) * ROWS + lax.broadcasted_iota(jnp.int32, (8, ROWS), 1)
    row_start[...] = starts_at(doc_ref, row_pos)


def prepare(doc_lengths, queries, own):
    vmem = pl.BlockSpec(memory_space=pltpu.VMEM)
    return pl.pallas_call(
        functools.partial(prepare_body, own),
        out_shape=(pltpu.VMEM((HEADS // 2 * WIDTH, 2 * ROWS), BF16), pltpu.VMEM((8, ROWS), jnp.int32)),
        in_specs=[pl.BlockSpec(memory_space=pltpu.SMEM), vmem],
        out_specs=(vmem, vmem),
        compiler_params=pltpu.CompilerParams(vmem_limit_bytes=4 << 20),
    )(doc_lengths, queries)


def attend_body(first, last, places, own, doc_ref, query, start_ref, *refs):
    kv_refs, refs = refs[: len(places)], refs[len(places) :]
    if not first:
        stat_in, acc_in, refs = refs[0], refs[1], refs[2:]
    if last:
        out, log_out, stat, acc, bias = refs
    else:
        stat, acc, bias = refs
    group, peer = own()
    q_first = (group * 4 + peer) * ROWS

    start_low = starts_at(doc_ref, q_first)
    start_high = starts_at(doc_ref, q_first + ROWS - 1)
    row_pos = q_first + lax.broadcasted_iota(jnp.int32, (1, ROWS), 1)
    row_start = start_ref[:1]
    span = BLOCKS * ROWS

    def pair_rows(values, h):
        return jnp.concatenate([values[h : h + 1], values[h + 1 : h + 2]], axis=1)

    def operands(tile):
        values = jnp.concatenate([tile[:, WIDTH:].T, jnp.ones((16, span), BF16)], axis=0)
        return tile[:, :WIDTH], values

    def set_bias(base):
        key_pos = base + lax.broadcasted_iota(jnp.int32, (span, ROWS), 0)
        hidden = jnp.where((key_pos >= row_start) & (key_pos <= row_pos), F32(0), F32(NEG))
        bias[:, :ROWS] = hidden
        bias[:, ROWS:] = hidden

    def exact(tile, base):
        keys, values = operands(tile)
        set_bias(base)

        for p in range(HEADS // 2):
            h = 2 * p
            score = jnp.dot(keys, query[p * WIDTH : (p + 1) * WIDTH], preferred_element_type=F32) * F32(SCALE) + bias[...]
            old = pair_rows(stat, h)
            new = jnp.maximum(old, jnp.max(score, axis=0, keepdims=True))
            fade = jnp.exp2(old - new)
            part = jnp.dot(values, jnp.exp2(score - new).astype(BF16), preferred_element_type=F32)
            for k in range(2):
                rows, cols = slice((h + k) * WIDTH, (h + k + 1) * WIDTH), slice(k * ROWS, (k + 1) * ROWS)
                acc[rows] = acc[rows] * fade[:, cols] + part[:WIDTH, cols]
                at = HEADS + h + k
                stat[at : at + 1] = stat[at : at + 1] * fade[:, cols] + part[WIDTH : WIDTH + 1, cols]
                stat[h + k : h + k + 1] = new[:, cols]

    def quick(tile, base, masked):
        keys, values = operands(tile)
        if masked:
            set_bias(base)
        for p in range(HEADS // 2):
            h = 2 * p
            held = pair_rows(stat, h)
            score = jnp.dot(keys, query[p * WIDTH : (p + 1) * WIDTH], preferred_element_type=F32) * F32(SCALE) - held
            if masked:
                score = score + bias[...]
            part = jnp.dot(values, jnp.exp2(score).astype(BF16), preferred_element_type=F32)
            for k in range(2):
                rows, cols = slice((h + k) * WIDTH, (h + k + 1) * WIDTH), slice(k * ROWS, (k + 1) * ROWS)
                acc[rows] += part[:WIDTH, cols]
                at = HEADS + h + k
                stat[at : at + 1] += part[WIDTH : WIDTH + 1, cols]

    def run(fast):
        if first:
            stat[:HEADS] = jnp.full((HEADS, ROWS), NEG, F32)
            stat[HEADS:] = jnp.zeros((HEADS, ROWS), F32)
            acc[...] = jnp.zeros_like(acc)
        else:
            stat[...] = stat_in[...]
            acc[...] = acc_in[...]

        for n, (kv_ref, (slots, place)) in enumerate(zip(kv_refs, places)):

            def body(i, _, kv_ref=kv_ref, place=place, own_tile=first and n == 0):
                load, tile_group = place(kv_ref, i, group)
                base = tile_group * span
                needed = (base + span > start_low) & (base < q_first + ROWS) & (base >= 0)
                whole = (base >= start_high) & (base + span <= q_first)
                if not fast:

                    @pl.when(needed)
                    def _():
                        exact(load(), base)

                    return 0

                @pl.when(needed & whole)
                def _():
                    quick(load(), base, False)

                @pl.when(needed & jnp.logical_not(whole))
                def _():
                    quick(load(), base, True)

                return 0

            start = 0
            if fast and first and n == 0:
                load, tile_group = place(kv_ref, 0, group)
                exact(load(), tile_group * span)
                start = 1
            lax.fori_loop(start, slots, body, 0)

    run(True)

    @pl.when(jnp.logical_not(jnp.max(stat[HEADS:]) <= F32(LIMIT)))
    def _():
        run(False)

    if last:
        stats = stat[...]
        for h in range(HEADS):
            rows = slice(h * WIDTH, (h + 1) * WIDTH)
            out[:, rows] = (acc[rows] / stats[HEADS + h : HEADS + h + 1]).T.astype(BF16)
        log_out[...] = stats[:HEADS] * F32(math.log(2.0)) + jnp.log(stats[HEADS:])


def attend(doc_lengths, prepared, pieces, state, last, own):
    places = [(kv.shape[1] // ROWS, place) for kv, place in pieces]
    vmem = pl.BlockSpec(memory_space=pltpu.VMEM)
    arrays = (*prepared, *(kv for kv, _ in pieces), *(state or ()))
    operands = [doc_lengths, *(pltpu.with_memory_space_constraint(a, pltpu.VMEM) for a in arrays)]
    state_shape = [(2 * HEADS, ROWS), (HEADS * WIDTH, ROWS)]
    bias = pltpu.VMEM((BLOCKS * ROWS, 2 * ROWS), F32)
    if last:
        out_shape = (
            jax.ShapeDtypeStruct((ROWS, HEADS * WIDTH), BF16),
            jax.ShapeDtypeStruct((HEADS, ROWS), F32),
        )
        scratch = [pltpu.VMEM(s, F32) for s in state_shape] + [bias]
    else:
        out_shape = tuple(pltpu.VMEM(s, F32) for s in state_shape)
        scratch = [bias]
    return pl.pallas_call(
        functools.partial(attend_body, state is None, last, places, own),
        out_shape=out_shape,
        in_specs=[pl.BlockSpec(memory_space=pltpu.SMEM)] + [vmem] * (len(operands) - 1),
        out_specs=(vmem, vmem),
        scratch_shapes=scratch,
        compiler_params=pltpu.CompilerParams(vmem_limit_bytes=16 << 20),
    )(*operands)


AXES = ("group", "peer")


def tiles(of_other, groups):
    def at(kv_ref, i, group):
        def load():
            return kv_ref[:, pl.ds(pl.multiple_of(i * ROWS, ROWS), ROWS), :].reshape(BLOCKS * ROWS, 2 * WIDTH)

        line, core = group // 2, group % 2
        return load, groups(i, line, 1 - core if of_other else core)

    return at


def near(i, line, core):
    pair = 2 * (line - 1 - core) + jnp.where(i == 1, core, 1 - core)
    return jnp.where(i == 0, 2 * line + core, pair)


def far(i, line, core):
    return 2 * (line - 3 - core) + jnp.where(i == 0, core, 1 - core)


def own():
    return lax.axis_index("group"), lax.axis_index("peer")


def moved(value, source):
    count = lax.axis_size("group") * lax.axis_size("peer")
    pairs = [(source(t), t) for t in range(count) if source(t) >= 0]
    return lax.ppermute(value, AXES, pairs)


def gathered(value):
    return lax.all_to_all(jnp.broadcast_to(value, (BLOCKS, *value.shape)), "peer", 0, 0)


def shards(queries, keys_values, doc_lengths):
    chip = jnp.concatenate([keys_values, moved(keys_values, lambda t: t ^ 4)], axis=0)
    pair_near = moved(chip, lambda t: t - 8 - 8 * (t // 4 % 2))
    pair_far = moved(chip, lambda t: t - 24 - 8 * (t // 4 % 2))
    prepared = prepare(doc_lengths, queries, own)
    near_mine = gathered(jnp.concatenate([keys_values, pair_near], axis=0))
    far_mine = gathered(pair_far)
    near_other = moved(near_mine, lambda t: t ^ 4)
    far_other = moved(far_mine, lambda t: t ^ 4)
    state = attend(doc_lengths, prepared, [(near_mine, tiles(False, near))], None, False, own)
    state = attend(
        doc_lengths, prepared, [(near_other, tiles(True, near)), (far_mine, tiles(False, far))], state, False, own
    )
    attended, log_total = attend(doc_lengths, prepared, [(far_other, tiles(True, far))], state, True, own)
    return attended, log_total.T


def solution(mesh):
    placed = (P(AXES, None), P(AXES, None), P())
    return jax.shard_map(shards, mesh=mesh, in_specs=placed, out_specs=(P(AXES, None), P(AXES, None)), check_vma=False)
```

```python
import functools
import math

import jax
import jax.numpy as jnp
from jax import lax
from jax.experimental import pallas as pl
from jax.experimental.pallas import tpu as pltpu
from jax.sharding import PartitionSpec as P


ROWS = 128
HEADS = 8
WIDTH = 128
BLOCKS = 4
NEG = -1e30
LIMIT = 2.0**40
SCALE = math.log2(math.e) / math.sqrt(WIDTH)
F32 = jnp.float32
BF16 = jnp.bfloat16


def starts_at(doc_ref, pos):
    def step(d, carry):
        end, start = carry
        end = end + doc_ref[d]
        return end, jnp.where(end <= pos, end, start)

    return lax.fori_loop(0, doc_ref.shape[0], step, (jnp.int32(0), jnp.zeros_like(pos)), unroll=True)[1]


def prepare_body(own, doc_ref, q_ref, query, row_start):
    for h in range(HEADS):
        rows = slice(h // 2 * WIDTH, (h // 2 + 1) * WIDTH)
        query[rows, h % 2 * ROWS : (h % 2 + 1) * ROWS] = q_ref[:, h * WIDTH : (h + 1) * WIDTH].T
    group, peer = own()
    row_pos = (group * 4 + peer) * ROWS + lax.broadcasted_iota(jnp.int32, (8, ROWS), 1)
    row_start[...] = starts_at(doc_ref, row_pos)


def prepare(doc_lengths, queries, own):
    vmem = pl.BlockSpec(memory_space=pltpu.VMEM)
    return pl.pallas_call(
        functools.partial(prepare_body, own),
        out_shape=(pltpu.VMEM((HEADS // 2 * WIDTH, 2 * ROWS), BF16), pltpu.VMEM((8, ROWS), jnp.int32)),
        in_specs=[pl.BlockSpec(memory_space=pltpu.SMEM), vmem],
        out_specs=(vmem, vmem),
        compiler_params=pltpu.CompilerParams(vmem_limit_bytes=4 << 20),
    )(doc_lengths, queries)


def attend_body(first, last, places, own, doc_ref, query, start_ref, *refs):
    kv_refs, refs = refs[: len(places)], refs[len(places) :]
    if not first:
        stat_in, acc_in, refs = refs[0], refs[1], refs[2:]
    if last:
        out, log_out, stat, acc, bias = refs
    else:
        stat, acc, bias = refs
    group, peer = own()
    q_first = (group * 4 + peer) * ROWS

    start_low = starts_at(doc_ref, q_first)
    start_high = starts_at(doc_ref, q_first + ROWS - 1)
    row_pos = q_first + lax.broadcasted_iota(jnp.int32, (1, ROWS), 1)
    row_start = start_ref[:1]
    span = BLOCKS * ROWS

    def pair_rows(values, h):
        return jnp.concatenate([values[h : h + 1], values[h + 1 : h + 2]], axis=1)

    def operands(tile):
        values = jnp.concatenate([tile[:, WIDTH:].T, jnp.ones((16, span), BF16)], axis=0)
        return tile[:, :WIDTH], values

    def set_bias(base, order):
        for n, place in enumerate(order):
            if not isinstance(order, range):
                place = (peer + place) % BLOCKS
            key_pos = base + place * ROWS + lax.broadcasted_iota(jnp.int32, (ROWS, ROWS), 0)
            hidden = jnp.where((key_pos >= row_start) & (key_pos <= row_pos), F32(0), F32(NEG))
            bias[n * ROWS : (n + 1) * ROWS, :ROWS] = hidden
            bias[n * ROWS : (n + 1) * ROWS, ROWS:] = hidden

    def exact(tile, base, order):
        keys, values = operands(tile)
        set_bias(base, order)

        for p in range(HEADS // 2):
            h = 2 * p
            score = jnp.dot(keys, query[p * WIDTH : (p + 1) * WIDTH], preferred_element_type=F32) * F32(SCALE) + bias[...]
            old = pair_rows(stat, h)
            new = jnp.maximum(old, jnp.max(score, axis=0, keepdims=True))
            fade = jnp.exp2(old - new)
            part = jnp.dot(values, jnp.exp2(score - new).astype(BF16), preferred_element_type=F32)
            for k in range(2):
                rows, cols = slice((h + k) * WIDTH, (h + k + 1) * WIDTH), slice(k * ROWS, (k + 1) * ROWS)
                acc[rows] = acc[rows] * fade[:, cols] + part[:WIDTH, cols]
                at = HEADS + h + k
                stat[at : at + 1] = stat[at : at + 1] * fade[:, cols] + part[WIDTH : WIDTH + 1, cols]
                stat[h + k : h + k + 1] = new[:, cols]

    def quick(tile, base, order, masked):
        keys, values = operands(tile)
        if masked:
            set_bias(base, order)
        for p in range(HEADS // 2):
            h = 2 * p
            held = pair_rows(stat, h)
            score = jnp.dot(keys, query[p * WIDTH : (p + 1) * WIDTH], preferred_element_type=F32) * F32(SCALE) - held
            if masked:
                score = score + bias[...]
            part = jnp.dot(values, jnp.exp2(score).astype(BF16), preferred_element_type=F32)
            for k in range(2):
                rows, cols = slice((h + k) * WIDTH, (h + k + 1) * WIDTH), slice(k * ROWS, (k + 1) * ROWS)
                acc[rows] += part[:WIDTH, cols]
                at = HEADS + h + k
                stat[at : at + 1] += part[WIDTH : WIDTH + 1, cols]

    def run(fast):
        if first:
            stat[:HEADS] = jnp.full((HEADS, ROWS), NEG, F32)
            stat[HEADS:] = jnp.zeros((HEADS, ROWS), F32)
            acc[...] = jnp.zeros_like(acc)
        else:
            stat[...] = stat_in[...]
            acc[...] = acc_in[...]

        for n, (kv_ref, (slots, place)) in enumerate(zip(kv_refs, places)):

            def body(i, _, kv_ref=kv_ref, place=place, own_tile=first and n == 0):
                load, tile_group, order = place(kv_ref, i, group)
                base = tile_group * span
                needed = (base + span > start_low) & (base < q_first + ROWS) & (base >= 0)
                whole = (base >= start_high) & (base + span <= q_first)
                if not fast:

                    @pl.when(needed)
                    def _():
                        exact(load(), base, order)

                    return 0

                @pl.when(needed & whole)
                def _():
                    quick(load(), base, order, False)

                @pl.when(needed & jnp.logical_not(whole))
                def _():
                    quick(load(), base, order, True)

                return 0

            start = 0
            if fast and first and n == 0:
                load, tile_group, order = place(kv_ref, 0, group)
                exact(load(), tile_group * span, order)
                start = 1
            lax.fori_loop(start, slots, body, 0)

    run(True)

    @pl.when(jnp.logical_not(jnp.max(stat[HEADS:]) <= F32(LIMIT)))
    def _():
        run(False)

    if last:
        stats = stat[...]
        for h in range(HEADS):
            rows = slice(h * WIDTH, (h + 1) * WIDTH)
            out[:, rows] = (acc[rows] / stats[HEADS + h : HEADS + h + 1]).T.astype(BF16)
        log_out[...] = stats[:HEADS] * F32(math.log(2.0)) + jnp.log(stats[HEADS:])


def attend(doc_lengths, prepared, pieces, state, last, own):
    places = [(kv.shape[1] // ROWS, place) for kv, place in pieces]
    vmem = pl.BlockSpec(memory_space=pltpu.VMEM)
    arrays = (*prepared, *(kv for kv, _ in pieces), *(state or ()))
    operands = [doc_lengths, *(pltpu.with_memory_space_constraint(a, pltpu.VMEM) for a in arrays)]
    state_shape = [(2 * HEADS, ROWS), (HEADS * WIDTH, ROWS)]
    bias = pltpu.VMEM((BLOCKS * ROWS, 2 * ROWS), F32)
    if last:
        out_shape = (
            jax.ShapeDtypeStruct((ROWS, HEADS * WIDTH), BF16),
            jax.ShapeDtypeStruct((HEADS, ROWS), F32),
        )
        scratch = [pltpu.VMEM(s, F32) for s in state_shape] + [bias]
    else:
        out_shape = tuple(pltpu.VMEM(s, F32) for s in state_shape)
        scratch = [bias]
    return pl.pallas_call(
        functools.partial(attend_body, state is None, last, places, own),
        out_shape=out_shape,
        in_specs=[pl.BlockSpec(memory_space=pltpu.SMEM)] + [vmem] * (len(operands) - 1),
        out_specs=(vmem, vmem),
        scratch_shapes=scratch,
        compiler_params=pltpu.CompilerParams(vmem_limit_bytes=16 << 20),
    )(*operands)


AXES = ("group", "peer")
TURNS = (0, 1, 3, 2)


def tiles(of_other, groups, turned=False):
    def at(kv_ref, i, group):
        def load():
            return kv_ref[:, pl.ds(pl.multiple_of(i * ROWS, ROWS), ROWS), :].reshape(BLOCKS * ROWS, 2 * WIDTH)

        line, core = group // 2, group % 2
        return load, groups(i, line, 1 - core if of_other else core), TURNS if turned else range(BLOCKS)

    return at


def near(i, line, core):
    pair = 2 * (line - 1 - core) + jnp.where(i == 1, core, 1 - core)
    return jnp.where(i == 0, 2 * line + core, pair)


def far(i, line, core):
    return 2 * (line - 3 - core) + jnp.where(i == 0, core, 1 - core)


def own():
    return lax.axis_index("group"), lax.axis_index("peer")


def moved(value, source):
    count = lax.axis_size("group") * lax.axis_size("peer")
    pairs = [(source(t), t) for t in range(count) if source(t) >= 0]
    return lax.ppermute(value, AXES, pairs)


def gathered(value):
    return lax.all_to_all(jnp.broadcast_to(value, (BLOCKS, *value.shape)), "peer", 0, 0)


def shards(queries, keys_values, doc_lengths):
    chip = jnp.concatenate([keys_values, moved(keys_values, lambda t: t ^ 4)], axis=0)
    pair_near = moved(chip, lambda t: t - 8 - 8 * (t // 4 % 2))
    pair_far = moved(chip, lambda t: t - 24 - 8 * (t // 4 % 2))
    prepared = prepare(doc_lengths, queries, own)
    near_mine = gathered(jnp.concatenate([keys_values, pair_near], axis=0))
    turns = []
    for k in (1, 3, 2):
        turns.append(moved(pair_far, lambda t, k=k: t // 4 * 4 + (t + k) % 4))
    far_mine = jnp.concatenate([pair_far, *turns], axis=0).reshape(BLOCKS, *pair_far.shape)
    near_other = moved(near_mine, lambda t: t ^ 4)
    far_other = moved(far_mine, lambda t: t ^ 4)
    state = attend(doc_lengths, prepared, [(near_mine, tiles(False, near))], None, False, own)
    state = attend(
        doc_lengths, prepared, [(near_other, tiles(True, near)), (far_mine, tiles(False, far, True))], state, False, own
    )
    attended, log_total = attend(doc_lengths, prepared, [(far_other, tiles(True, far, True))], state, True, own)
    return attended, log_total.T


def solution(mesh):
    placed = (P(AXES, None), P(AXES, None), P())
    return jax.shard_map(shards, mesh=mesh, in_specs=placed, out_specs=(P(AXES, None), P(AXES, None)), check_vma=False)
```

```python
import functools
import math

import jax
import jax.numpy as jnp
from jax import lax
from jax.experimental import pallas as pl
from jax.experimental.pallas import tpu as pltpu
from jax.sharding import PartitionSpec as P


ROWS = 128
HEADS = 8
WIDTH = 128
BLOCKS = 4
NEG = -1e30
LIMIT = 2.0**40
SCALE = math.log2(math.e) / math.sqrt(WIDTH)
F32 = jnp.float32
BF16 = jnp.bfloat16


def starts_at(doc_ref, pos):
    def step(d, carry):
        end, start = carry
        end = end + doc_ref[d]
        return end, jnp.where(end <= pos, end, start)

    return lax.fori_loop(0, doc_ref.shape[0], step, (jnp.int32(0), jnp.zeros_like(pos)), unroll=True)[1]


def starts_body(own, doc_ref, row_start):
    group, peer = own()
    row_pos = (group * 4 + peer) * ROWS + lax.broadcasted_iota(jnp.int32, (8, ROWS), 1)
    row_start[...] = starts_at(doc_ref, row_pos)


def row_starts(doc_lengths, own):
    return pl.pallas_call(
        functools.partial(starts_body, own),
        out_shape=pltpu.VMEM((8, ROWS), jnp.int32),
        in_specs=[pl.BlockSpec(memory_space=pltpu.SMEM)],
        out_specs=pl.BlockSpec(memory_space=pltpu.VMEM),
        compiler_params=pltpu.CompilerParams(vmem_limit_bytes=4 << 20),
    )(doc_lengths)


def pairs_body(q_ref, query):
    for h in range(HEADS):
        rows = slice(h // 2 * WIDTH, (h // 2 + 1) * WIDTH)
        query[rows, h % 2 * ROWS : (h % 2 + 1) * ROWS] = q_ref[:, h * WIDTH : (h + 1) * WIDTH].T


def query_pairs(queries):
    vmem = pl.BlockSpec(memory_space=pltpu.VMEM)
    return pl.pallas_call(
        pairs_body,
        out_shape=pltpu.VMEM((HEADS // 2 * WIDTH, 2 * ROWS), BF16),
        in_specs=[vmem],
        out_specs=vmem,
        compiler_params=pltpu.CompilerParams(vmem_limit_bytes=4 << 20),
    )(queries)


def spread_body(*refs):
    out, at = refs[-1], 0
    for ref in refs[:-1]:
        value = ref[...]
        for n in range(BLOCKS):
            out[n, at : at + value.shape[0]] = value
        at += value.shape[0]


def spread(*values):
    vmem = pl.BlockSpec(memory_space=pltpu.VMEM)
    rows = sum(v.shape[0] for v in values)
    return pl.pallas_call(
        spread_body,
        out_shape=pltpu.VMEM((BLOCKS, rows, 2 * WIDTH), BF16),
        in_specs=[vmem] * len(values),
        out_specs=vmem,
        compiler_params=pltpu.CompilerParams(vmem_limit_bytes=4 << 20),
    )(*(pltpu.with_memory_space_constraint(v, pltpu.VMEM) for v in values))


def attend_body(first, last, places, own, doc_ref, query, start_ref, *refs):
    kv_refs, refs = refs[: len(places)], refs[len(places) :]
    if not first:
        stat_in, acc_in, refs = refs[0], refs[1], refs[2:]
    if last:
        out, log_out, stat, acc, bias = refs
    else:
        stat, acc, bias = refs
    group, peer = own()
    q_first = (group * 4 + peer) * ROWS

    start_low = starts_at(doc_ref, q_first)
    start_high = starts_at(doc_ref, q_first + ROWS - 1)
    row_pos = q_first + lax.broadcasted_iota(jnp.int32, (1, ROWS), 1)
    row_start = start_ref[:1]
    span = BLOCKS * ROWS

    def pair_rows(values, h):
        return jnp.concatenate([values[h : h + 1], values[h + 1 : h + 2]], axis=1)

    def operands(tile):
        values = jnp.concatenate([tile[:, WIDTH:].T, jnp.ones((16, span), BF16)], axis=0)
        return tile[:, :WIDTH], values

    def set_bias(base, order):
        for n, place in enumerate(order):
            if not isinstance(order, range):
                place = (peer + place) % BLOCKS
            key_pos = base + place * ROWS + lax.broadcasted_iota(jnp.int32, (ROWS, ROWS), 0)
            hidden = jnp.where((key_pos >= row_start) & (key_pos <= row_pos), F32(0), F32(NEG))
            bias[n * ROWS : (n + 1) * ROWS, :ROWS] = hidden
            bias[n * ROWS : (n + 1) * ROWS, ROWS:] = hidden

    def exact(tile, base, order):
        keys, values = operands(tile)
        set_bias(base, order)

        for p in range(HEADS // 2):
            h = 2 * p
            score = jnp.dot(keys, query[p * WIDTH : (p + 1) * WIDTH], preferred_element_type=F32) * F32(SCALE) + bias[...]
            old = pair_rows(stat, h)
            new = jnp.maximum(old, jnp.max(score, axis=0, keepdims=True))
            fade = jnp.exp2(old - new)
            part = jnp.dot(values, jnp.exp2(score - new).astype(BF16), preferred_element_type=F32)
            for k in range(2):
                rows, cols = slice((h + k) * WIDTH, (h + k + 1) * WIDTH), slice(k * ROWS, (k + 1) * ROWS)
                acc[rows] = acc[rows] * fade[:, cols] + part[:WIDTH, cols]
                at = HEADS + h + k
                stat[at : at + 1] = stat[at : at + 1] * fade[:, cols] + part[WIDTH : WIDTH + 1, cols]
                stat[h + k : h + k + 1] = new[:, cols]

    def quick(tile, base, order, masked):
        keys, values = operands(tile)
        if masked:
            set_bias(base, order)
        for p in range(HEADS // 2):
            h = 2 * p
            held = pair_rows(stat, h)
            score = jnp.dot(keys, query[p * WIDTH : (p + 1) * WIDTH], preferred_element_type=F32) * F32(SCALE) - held
            if masked:
                score = score + bias[...]
            part = jnp.dot(values, jnp.exp2(score).astype(BF16), preferred_element_type=F32)
            for k in range(2):
                rows, cols = slice((h + k) * WIDTH, (h + k + 1) * WIDTH), slice(k * ROWS, (k + 1) * ROWS)
                acc[rows] += part[:WIDTH, cols]
                at = HEADS + h + k
                stat[at : at + 1] += part[WIDTH : WIDTH + 1, cols]

    def run(fast):
        if first:
            stat[:HEADS] = jnp.full((HEADS, ROWS), NEG, F32)
            stat[HEADS:] = jnp.zeros((HEADS, ROWS), F32)
            acc[...] = jnp.zeros_like(acc)
        else:
            stat[...] = stat_in[...]
            acc[...] = acc_in[...]

        for n, (kv_ref, (slots, place)) in enumerate(zip(kv_refs, places)):

            def body(i, _, kv_ref=kv_ref, place=place, own_tile=first and n == 0):
                load, tile_group, order = place(kv_ref, i, group)
                base = tile_group * span
                needed = (base + span > start_low) & (base < q_first + ROWS) & (base >= 0)
                whole = (base >= start_high) & (base + span <= q_first)
                if not fast:

                    @pl.when(needed)
                    def _():
                        exact(load(), base, order)

                    return 0

                @pl.when(needed & whole)
                def _():
                    quick(load(), base, order, False)

                @pl.when(needed & jnp.logical_not(whole))
                def _():
                    quick(load(), base, order, True)

                return 0

            start = 0
            if fast and first and n == 0:
                load, tile_group, order = place(kv_ref, 0, group)
                exact(load(), tile_group * span, order)
                start = 1
            lax.fori_loop(start, slots, body, 0)

    run(True)

    @pl.when(jnp.logical_not(jnp.max(stat[HEADS:]) <= F32(LIMIT)))
    def _():
        run(False)

    if last:
        stats = stat[...]
        for h in range(HEADS):
            rows = slice(h * WIDTH, (h + 1) * WIDTH)
            out[:, rows] = (acc[rows] / stats[HEADS + h : HEADS + h + 1]).T.astype(BF16)
        log_out[...] = stats[:HEADS] * F32(math.log(2.0)) + jnp.log(stats[HEADS:])


def attend(doc_lengths, prepared, pieces, state, last, own):
    places = [(kv.shape[1] // ROWS, place) for kv, place in pieces]
    vmem = pl.BlockSpec(memory_space=pltpu.VMEM)
    arrays = (*prepared, *(kv for kv, _ in pieces), *(state or ()))
    operands = [doc_lengths, *(pltpu.with_memory_space_constraint(a, pltpu.VMEM) for a in arrays)]
    state_shape = [(2 * HEADS, ROWS), (HEADS * WIDTH, ROWS)]
    bias = pltpu.VMEM((BLOCKS * ROWS, 2 * ROWS), F32)
    if last:
        out_shape = (
            jax.ShapeDtypeStruct((ROWS, HEADS * WIDTH), BF16),
            jax.ShapeDtypeStruct((HEADS, ROWS), F32),
        )
        scratch = [pltpu.VMEM(s, F32) for s in state_shape] + [bias]
    else:
        out_shape = tuple(pltpu.VMEM(s, F32) for s in state_shape)
        scratch = [bias]
    return pl.pallas_call(
        functools.partial(attend_body, state is None, last, places, own),
        out_shape=out_shape,
        in_specs=[pl.BlockSpec(memory_space=pltpu.SMEM)] + [vmem] * (len(operands) - 1),
        out_specs=(vmem, vmem),
        scratch_shapes=scratch,
        compiler_params=pltpu.CompilerParams(vmem_limit_bytes=16 << 20),
    )(*operands)


AXES = ("group", "peer")
TURNS = (0, 1, 3, 2)


def tiles(of_other, groups, turned=False):
    def at(kv_ref, i, group):
        def load():
            return kv_ref[:, pl.ds(pl.multiple_of(i * ROWS, ROWS), ROWS), :].reshape(BLOCKS * ROWS, 2 * WIDTH)

        line, core = group // 2, group % 2
        return load, groups(i, line, 1 - core if of_other else core), TURNS if turned else range(BLOCKS)

    return at


def near(i, line, core):
    pair = 2 * (line - 1 - core) + jnp.where(i == 1, core, 1 - core)
    return jnp.where(i == 0, 2 * line + core, pair)


def far(i, line, core):
    return 2 * (line - 3 - core) + jnp.where(i == 0, core, 1 - core)


def own():
    return lax.axis_index("group"), lax.axis_index("peer")


def moved(value, source):
    count = lax.axis_size("group") * lax.axis_size("peer")
    pairs = [(source(t), t) for t in range(count) if source(t) >= 0]
    return lax.ppermute(value, AXES, pairs)


def shards(queries, keys_values, doc_lengths):
    chip = jnp.concatenate([keys_values, moved(keys_values, lambda t: t ^ 4)], axis=0)
    pair_near = moved(chip, lambda t: t - 8 - 8 * (t // 4 % 2))
    pair_far = moved(chip, lambda t: t - 24 - 8 * (t // 4 % 2))
    starts = row_starts(doc_lengths, own)
    prepared = query_pairs(queries), starts
    near_mine = lax.all_to_all(spread(keys_values, pair_near), "peer", 0, 0)
    turns = []
    for k in (1, 3, 2):
        turns.append(moved(pair_far, lambda t, k=k: t // 4 * 4 + (t + k) % 4))
    far_mine = jnp.concatenate([pair_far, *turns], axis=0).reshape(BLOCKS, *pair_far.shape)
    near_other = moved(near_mine, lambda t: t ^ 4)
    far_other = moved(far_mine, lambda t: t ^ 4)
    state = attend(doc_lengths, prepared, [(near_mine, tiles(False, near))], None, False, own)
    state = attend(
        doc_lengths, prepared, [(near_other, tiles(True, near)), (far_mine, tiles(False, far, True))], state, False, own
    )
    attended, log_total = attend(doc_lengths, prepared, [(far_other, tiles(True, far, True))], state, True, own)
    return attended, log_total.T


def solution(mesh):
    placed = (P(AXES, None), P(AXES, None), P())
    return jax.shard_map(shards, mesh=mesh, in_specs=placed, out_specs=(P(AXES, None), P(AXES, None)), check_vma=False)
```

```python
import functools
import math

import jax
import jax.numpy as jnp
from jax import lax
from jax.experimental import pallas as pl
from jax.experimental.pallas import tpu as pltpu
from jax.sharding import PartitionSpec as P


ROWS = 128
HEADS = 8
WIDTH = 128
BLOCKS = 4
CHUNK = 256
NEG = -1e30
LIMIT = 2.0**40
SCALE = math.log2(math.e) / math.sqrt(WIDTH)
F32 = jnp.float32
BF16 = jnp.bfloat16


def starts_at(doc_ref, pos):
    def step(d, carry):
        end, start = carry
        end = end + doc_ref[d]
        return end, jnp.where(end <= pos, end, start)

    return lax.fori_loop(0, doc_ref.shape[0], step, (jnp.int32(0), jnp.zeros_like(pos)), unroll=True)[1]


def starts_body(own, doc_ref, row_start):
    group, peer = own()
    row_pos = (group * 4 + peer) * ROWS + lax.broadcasted_iota(jnp.int32, (8, ROWS), 1)
    row_start[...] = starts_at(doc_ref, row_pos)


def row_starts(doc_lengths, own):
    return pl.pallas_call(
        functools.partial(starts_body, own),
        out_shape=pltpu.VMEM((8, ROWS), jnp.int32),
        in_specs=[pl.BlockSpec(memory_space=pltpu.SMEM)],
        out_specs=pl.BlockSpec(memory_space=pltpu.VMEM),
        compiler_params=pltpu.CompilerParams(vmem_limit_bytes=4 << 20),
    )(doc_lengths)


def pairs_body(q_ref, query):
    for h in range(HEADS):
        rows = slice(h // 2 * WIDTH, (h // 2 + 1) * WIDTH)
        query[rows, h % 2 * ROWS : (h % 2 + 1) * ROWS] = q_ref[:, h * WIDTH : (h + 1) * WIDTH].T


def query_pairs(queries):
    vmem = pl.BlockSpec(memory_space=pltpu.VMEM)
    return pl.pallas_call(
        pairs_body,
        out_shape=pltpu.VMEM((HEADS // 2 * WIDTH, 2 * ROWS), BF16),
        in_specs=[vmem],
        out_specs=vmem,
        compiler_params=pltpu.CompilerParams(vmem_limit_bytes=4 << 20),
    )(queries)


def spread_body(*refs):
    out, at = refs[-1], 0
    for ref in refs[:-1]:
        value = ref[...]
        for n in range(BLOCKS):
            out[n, at : at + value.shape[0]] = value
        at += value.shape[0]


def spread(*values):
    vmem = pl.BlockSpec(memory_space=pltpu.VMEM)
    rows = sum(v.shape[0] for v in values)
    return pl.pallas_call(
        spread_body,
        out_shape=pltpu.VMEM((BLOCKS, rows, 2 * WIDTH), BF16),
        in_specs=[vmem] * len(values),
        out_specs=vmem,
        compiler_params=pltpu.CompilerParams(vmem_limit_bytes=4 << 20),
    )(*(pltpu.with_memory_space_constraint(v, pltpu.VMEM) for v in values))


def attend_body(first, last, places, own, doc_ref, query, start_ref, *refs):
    kv_refs, refs = refs[: len(places)], refs[len(places) :]
    if not first:
        stat_in, acc_in, refs = refs[0], refs[1], refs[2:]
    if last:
        out, log_out, stat, acc, bias = refs
    else:
        stat, acc, bias = refs
    group, peer = own()
    q_first = (group * 4 + peer) * ROWS

    start_low = starts_at(doc_ref, q_first)
    start_high = starts_at(doc_ref, q_first + ROWS - 1)
    row_pos = q_first + lax.broadcasted_iota(jnp.int32, (1, ROWS), 1)
    row_start = start_ref[:1]
    span = BLOCKS * ROWS

    def pair_rows(values, h):
        return jnp.concatenate([values[h : h + 1], values[h + 1 : h + 2]], axis=1)

    def operands(tile):
        values = jnp.concatenate([tile[:, WIDTH:].T, jnp.ones((16, span), BF16)], axis=0)
        return tile[:, :WIDTH], values

    def set_bias(base, order):
        for n, place in enumerate(order):
            if not isinstance(order, range):
                place = (peer + place) % BLOCKS
            key_pos = base + place * ROWS + lax.broadcasted_iota(jnp.int32, (ROWS, ROWS), 0)
            hidden = jnp.where((key_pos >= row_start) & (key_pos <= row_pos), F32(0), F32(NEG))
            bias[n * ROWS : (n + 1) * ROWS, :ROWS] = hidden
            bias[n * ROWS : (n + 1) * ROWS, ROWS:] = hidden

    def exact(tile, base, order):
        keys, values = operands(tile)
        set_bias(base, order)

        for p in range(HEADS // 2):
            h = 2 * p
            score = jnp.dot(keys, query[p * WIDTH : (p + 1) * WIDTH], preferred_element_type=F32) * F32(SCALE) + bias[...]
            old = pair_rows(stat, h)
            new = jnp.maximum(old, jnp.max(score, axis=0, keepdims=True))
            fade = jnp.exp2(old - new)
            part = jnp.dot(values, jnp.exp2(score - new).astype(BF16), preferred_element_type=F32)
            for k in range(2):
                rows, cols = slice((h + k) * WIDTH, (h + k + 1) * WIDTH), slice(k * ROWS, (k + 1) * ROWS)
                acc[rows] = acc[rows] * fade[:, cols] + part[:WIDTH, cols]
                at = HEADS + h + k
                stat[at : at + 1] = stat[at : at + 1] * fade[:, cols] + part[WIDTH : WIDTH + 1, cols]
                stat[h + k : h + k + 1] = new[:, cols]

    def quick(tile, base, order, masked):
        keys, values = operands(tile)
        if masked:
            set_bias(base, order)
        for p in range(HEADS // 2):
            h = 2 * p
            held = pair_rows(stat, h)
            part = None
            for c in range(0, span, CHUNK):
                score = jnp.dot(
                    keys[c : c + CHUNK], query[p * WIDTH : (p + 1) * WIDTH], preferred_element_type=F32
                ) * F32(SCALE) - held
                if masked:
                    score = score + bias[c : c + CHUNK]
                weight = jnp.exp2(score).astype(BF16)
                piece = jnp.dot(values[:, c : c + CHUNK], weight, preferred_element_type=F32)
                part = piece if part is None else part + piece
            for k in range(2):
                rows, cols = slice((h + k) * WIDTH, (h + k + 1) * WIDTH), slice(k * ROWS, (k + 1) * ROWS)
                acc[rows] += part[:WIDTH, cols]
                at = HEADS + h + k
                stat[at : at + 1] += part[WIDTH : WIDTH + 1, cols]

    def run(fast):
        if first:
            stat[:HEADS] = jnp.full((HEADS, ROWS), NEG, F32)
            stat[HEADS:] = jnp.zeros((HEADS, ROWS), F32)
            acc[...] = jnp.zeros_like(acc)
        else:
            stat[...] = stat_in[...]
            acc[...] = acc_in[...]

        for n, (kv_ref, (slots, place)) in enumerate(zip(kv_refs, places)):

            def body(i, _, kv_ref=kv_ref, place=place, own_tile=first and n == 0):
                load, tile_group, order = place(kv_ref, i, group)
                base = tile_group * span
                needed = (base + span > start_low) & (base < q_first + ROWS) & (base >= 0)
                whole = (base >= start_high) & (base + span <= q_first)
                if not fast:

                    @pl.when(needed)
                    def _():
                        exact(load(), base, order)

                    return 0

                @pl.when(needed & whole)
                def _():
                    quick(load(), base, order, False)

                @pl.when(needed & jnp.logical_not(whole))
                def _():
                    quick(load(), base, order, True)

                return 0

            start = 0
            if fast and first and n == 0:
                load, tile_group, order = place(kv_ref, 0, group)
                exact(load(), tile_group * span, order)
                start = 1
            lax.fori_loop(start, slots, body, 0)

    run(True)

    @pl.when(jnp.logical_not(jnp.max(stat[HEADS:]) <= F32(LIMIT)))
    def _():
        run(False)

    if last:
        stats = stat[...]
        for h in range(HEADS):
            rows = slice(h * WIDTH, (h + 1) * WIDTH)
            out[:, rows] = (acc[rows] / stats[HEADS + h : HEADS + h + 1]).T.astype(BF16)
        log_out[...] = stats[:HEADS] * F32(math.log(2.0)) + jnp.log(stats[HEADS:])


def attend(doc_lengths, prepared, pieces, state, last, own):
    places = [(kv.shape[1] // ROWS, place) for kv, place in pieces]
    vmem = pl.BlockSpec(memory_space=pltpu.VMEM)
    arrays = (*prepared, *(kv for kv, _ in pieces), *(state or ()))
    operands = [doc_lengths, *(pltpu.with_memory_space_constraint(a, pltpu.VMEM) for a in arrays)]
    state_shape = [(2 * HEADS, ROWS), (HEADS * WIDTH, ROWS)]
    bias = pltpu.VMEM((BLOCKS * ROWS, 2 * ROWS), F32)
    if last:
        out_shape = (
            jax.ShapeDtypeStruct((ROWS, HEADS * WIDTH), BF16),
            jax.ShapeDtypeStruct((HEADS, ROWS), F32),
        )
        scratch = [pltpu.VMEM(s, F32) for s in state_shape] + [bias]
    else:
        out_shape = tuple(pltpu.VMEM(s, F32) for s in state_shape)
        scratch = [bias]
    return pl.pallas_call(
        functools.partial(attend_body, state is None, last, places, own),
        out_shape=out_shape,
        in_specs=[pl.BlockSpec(memory_space=pltpu.SMEM)] + [vmem] * (len(operands) - 1),
        out_specs=(vmem, vmem),
        scratch_shapes=scratch,
        compiler_params=pltpu.CompilerParams(vmem_limit_bytes=16 << 20),
    )(*operands)


AXES = ("group", "peer")
TURNS = (0, 1, 3, 2)


def tiles(of_other, back, turned=False):
    def at(kv_ref, i, group):
        def load():
            return kv_ref[:, pl.ds(pl.multiple_of(i * ROWS, ROWS), ROWS), :].reshape(BLOCKS * ROWS, 2 * WIDTH)

        line, core = group // 2, group % 2
        if of_other:
            core = 1 - core
        order = TURNS if turned else range(BLOCKS)
        if not back:
            return load, 2 * line + core, order
        return load, 2 * (line - back - core) + jnp.where(i == 0, core, 1 - core), order

    return at


def own():
    return lax.axis_index("group"), lax.axis_index("peer")


def moved(value, source):
    count = lax.axis_size("group") * lax.axis_size("peer")
    pairs = [(source(t), t) for t in range(count) if source(t) >= 0]
    return lax.ppermute(value, AXES, pairs)


def across(value):
    return lax.all_to_all(value, "peer", 0, 0)


def swapped(value):
    return moved(value, lambda t: t ^ 4)


def shards(queries, keys_values, doc_lengths):
    chip = jnp.concatenate([keys_values, swapped(keys_values)], axis=0)
    pair_near = moved(chip, lambda t: t - 8 - 8 * (t // 4 % 2))
    own_mine = across(spread(keys_values))
    own_other = swapped(own_mine)
    pair_far = moved(chip, lambda t: t - 24 - 8 * (t // 4 % 2))
    starts = row_starts(doc_lengths, own)
    prepared = query_pairs(queries), starts

    def step(pieces, state, last=False):
        return attend(doc_lengths, prepared, pieces, state, last, own)

    state = step([(own_mine, tiles(False, 0)), (own_other, tiles(True, 0))], None)
    near_mine = across(spread(pair_near))
    turns = []
    for k in (1, 3, 2):
        turns.append(moved(pair_far, lambda t, k=k: t // 4 * 4 + (t + k) % 4))
    far_mine = jnp.concatenate([pair_far, *turns], axis=0).reshape(BLOCKS, *pair_far.shape)
    near_other = swapped(near_mine)
    state = step([(near_mine, tiles(False, 1))], state)
    far_other = swapped(far_mine)
    state = step([(near_other, tiles(True, 1)), (far_mine, tiles(False, 3, True))], state)
    attended, log_total = step([(far_other, tiles(True, 3, True))], state, True)
    return attended, log_total.T


def solution(mesh):
    placed = (P(AXES, None), P(AXES, None), P())
    return jax.shard_map(shards, mesh=mesh, in_specs=placed, out_specs=(P(AXES, None), P(AXES, None)), check_vma=False)
```

```python
import functools
import math

import jax
import jax.numpy as jnp
from jax import lax
from jax.experimental import pallas as pl
from jax.experimental.pallas import tpu as pltpu
from jax.sharding import PartitionSpec as P


ROWS = 128
HEADS = 8
WIDTH = 128
BLOCKS = 4
CHUNK = 256
NEG = -1e30
LIMIT = 2.0**40
SCALE = math.log2(math.e) / math.sqrt(WIDTH)
F32 = jnp.float32
BF16 = jnp.bfloat16


def starts_at(doc_ref, pos):
    def step(d, carry):
        end, start = carry
        end = end + doc_ref[d]
        return end, jnp.where(end <= pos, end, start)

    return lax.fori_loop(0, doc_ref.shape[0], step, (jnp.int32(0), jnp.zeros_like(pos)), unroll=True)[1]


def starts_body(own, doc_ref, row_start):
    group, peer = own()
    row_pos = (group * 4 + peer) * ROWS + lax.broadcasted_iota(jnp.int32, (8, ROWS), 1)
    row_start[...] = starts_at(doc_ref, row_pos)


def row_starts(doc_lengths, own):
    return pl.pallas_call(
        functools.partial(starts_body, own),
        out_shape=pltpu.VMEM((8, ROWS), jnp.int32),
        in_specs=[pl.BlockSpec(memory_space=pltpu.SMEM)],
        out_specs=pl.BlockSpec(memory_space=pltpu.VMEM),
        compiler_params=pltpu.CompilerParams(vmem_limit_bytes=4 << 20),
    )(doc_lengths)


def pairs_body(q_ref, query):
    for h in range(HEADS):
        rows = slice(h // 2 * WIDTH, (h // 2 + 1) * WIDTH)
        query[rows, h % 2 * ROWS : (h % 2 + 1) * ROWS] = q_ref[:, h * WIDTH : (h + 1) * WIDTH].T


def query_pairs(queries):
    vmem = pl.BlockSpec(memory_space=pltpu.VMEM)
    return pl.pallas_call(
        pairs_body,
        out_shape=pltpu.VMEM((HEADS // 2 * WIDTH, 2 * ROWS), BF16),
        in_specs=[vmem],
        out_specs=vmem,
        compiler_params=pltpu.CompilerParams(vmem_limit_bytes=4 << 20),
    )(queries)


def spread_body(*refs):
    out, at = refs[-1], 0
    for ref in refs[:-1]:
        value = ref[...]
        for n in range(BLOCKS):
            out[n, at : at + value.shape[0]] = value
        at += value.shape[0]


def spread(*values):
    vmem = pl.BlockSpec(memory_space=pltpu.VMEM)
    rows = sum(v.shape[0] for v in values)
    return pl.pallas_call(
        spread_body,
        out_shape=pltpu.VMEM((BLOCKS, rows, 2 * WIDTH), BF16),
        in_specs=[vmem] * len(values),
        out_specs=vmem,
        compiler_params=pltpu.CompilerParams(vmem_limit_bytes=4 << 20),
    )(*(pltpu.with_memory_space_constraint(v, pltpu.VMEM) for v in values))


def attend_body(first, last, places, own, doc_ref, query, start_ref, *refs):
    kv_refs, refs = refs[: len(places)], refs[len(places) :]
    if not first:
        stat_in, acc_in, refs = refs[0], refs[1], refs[2:]
    if last:
        out, log_out, stat, acc, bias = refs
    else:
        stat, acc, bias = refs
    group, peer = own()
    q_first = (group * 4 + peer) * ROWS

    start_low = starts_at(doc_ref, q_first)
    start_high = starts_at(doc_ref, q_first + ROWS - 1)
    row_pos = q_first + lax.broadcasted_iota(jnp.int32, (1, ROWS), 1)
    row_start = start_ref[:1]
    span = BLOCKS * ROWS

    def pair_rows(values, h):
        return jnp.concatenate([values[h : h + 1], values[h + 1 : h + 2]], axis=1)

    def operands(tile):
        values = jnp.concatenate([tile[:, WIDTH:].T, jnp.ones((16, span), BF16)], axis=0)
        return tile[:, :WIDTH], values

    def set_bias(base):
        key_pos = base + lax.broadcasted_iota(jnp.int32, (span, ROWS), 0)
        hidden = jnp.where((key_pos >= row_start) & (key_pos <= row_pos), F32(0), F32(NEG))
        bias[:, :ROWS] = hidden
        bias[:, ROWS:] = hidden

    def exact(tile, base):
        keys, values = operands(tile)
        set_bias(base)

        for p in range(HEADS // 2):
            h = 2 * p
            score = jnp.dot(keys, query[p * WIDTH : (p + 1) * WIDTH], preferred_element_type=F32) * F32(SCALE) + bias[...]
            old = pair_rows(stat, h)
            new = jnp.maximum(old, jnp.max(score, axis=0, keepdims=True))
            fade = jnp.exp2(old - new)
            part = jnp.dot(values, jnp.exp2(score - new).astype(BF16), preferred_element_type=F32)
            for k in range(2):
                rows, cols = slice((h + k) * WIDTH, (h + k + 1) * WIDTH), slice(k * ROWS, (k + 1) * ROWS)
                acc[rows] = acc[rows] * fade[:, cols] + part[:WIDTH, cols]
                at = HEADS + h + k
                stat[at : at + 1] = stat[at : at + 1] * fade[:, cols] + part[WIDTH : WIDTH + 1, cols]
                stat[h + k : h + k + 1] = new[:, cols]

    def quick(tile, base, masked):
        keys, values = operands(tile)
        if masked:
            set_bias(base)
        for p in range(HEADS // 2):
            h = 2 * p
            held = pair_rows(stat, h)
            part = None
            for c in range(0, span, CHUNK):
                score = jnp.dot(
                    keys[c : c + CHUNK], query[p * WIDTH : (p + 1) * WIDTH], preferred_element_type=F32
                ) * F32(SCALE) - held
                if masked:
                    score = score + bias[c : c + CHUNK]
                weight = jnp.exp2(score).astype(BF16)
                piece = jnp.dot(values[:, c : c + CHUNK], weight, preferred_element_type=F32)
                part = piece if part is None else part + piece
            for k in range(2):
                rows, cols = slice((h + k) * WIDTH, (h + k + 1) * WIDTH), slice(k * ROWS, (k + 1) * ROWS)
                acc[rows] += part[:WIDTH, cols]
                at = HEADS + h + k
                stat[at : at + 1] += part[WIDTH : WIDTH + 1, cols]

    def run(fast):
        if first:
            stat[:HEADS] = jnp.full((HEADS, ROWS), NEG, F32)
            stat[HEADS:] = jnp.zeros((HEADS, ROWS), F32)
            acc[...] = jnp.zeros_like(acc)
        else:
            stat[...] = stat_in[...]
            acc[...] = acc_in[...]

        for n, (kv_ref, (slots, place)) in enumerate(zip(kv_refs, places)):

            def body(i, _, kv_ref=kv_ref, place=place, own_tile=first and n == 0):
                load, tile_group = place(kv_ref, i, group)
                base = tile_group * span
                needed = (base + span > start_low) & (base < q_first + ROWS) & (base >= 0)
                whole = (base >= start_high) & (base + span <= q_first)
                if not fast:

                    @pl.when(needed)
                    def _():
                        exact(load(), base)

                    return 0

                @pl.when(needed & whole)
                def _():
                    quick(load(), base, False)

                @pl.when(needed & jnp.logical_not(whole))
                def _():
                    quick(load(), base, True)

                return 0

            start = 0
            if fast and first and n == 0:
                load, tile_group = place(kv_ref, 0, group)
                exact(load(), tile_group * span)
                start = 1
            lax.fori_loop(start, slots, body, 0)

    run(True)

    @pl.when(jnp.logical_not(jnp.max(stat[HEADS:]) <= F32(LIMIT)))
    def _():
        run(False)

    if last:
        stats = stat[...]
        inverse = 1.0 / stats[HEADS:]
        for h in range(HEADS):
            rows = slice(h * WIDTH, (h + 1) * WIDTH)
            out[:, rows] = (acc[rows] * inverse[h : h + 1]).T.astype(BF16)
        log_out[...] = stats[:HEADS] * F32(math.log(2.0)) + jnp.log(stats[HEADS:])


def attend(doc_lengths, prepared, pieces, state, last, own):
    places = [(kv.shape[1] // ROWS, place) for kv, place in pieces]
    vmem = pl.BlockSpec(memory_space=pltpu.VMEM)
    arrays = (*prepared, *(kv for kv, _ in pieces), *(state or ()))
    operands = [doc_lengths, *(pltpu.with_memory_space_constraint(a, pltpu.VMEM) for a in arrays)]
    state_shape = [(2 * HEADS, ROWS), (HEADS * WIDTH, ROWS)]
    bias = pltpu.VMEM((BLOCKS * ROWS, 2 * ROWS), F32)
    if last:
        out_shape = (
            jax.ShapeDtypeStruct((ROWS, HEADS * WIDTH), BF16),
            jax.ShapeDtypeStruct((HEADS, ROWS), F32),
        )
        scratch = [pltpu.VMEM(s, F32) for s in state_shape] + [bias]
    else:
        out_shape = tuple(pltpu.VMEM(s, F32) for s in state_shape)
        scratch = [bias]
    return pl.pallas_call(
        functools.partial(attend_body, state is None, last, places, own),
        out_shape=out_shape,
        in_specs=[pl.BlockSpec(memory_space=pltpu.SMEM)] + [vmem] * (len(operands) - 1),
        out_specs=(vmem, vmem),
        scratch_shapes=scratch,
        compiler_params=pltpu.CompilerParams(vmem_limit_bytes=16 << 20),
    )(*operands)


AXES = ("group", "peer")


def tiles(of_other, back):
    def at(kv_ref, i, group):
        def load():
            return kv_ref[:, pl.ds(pl.multiple_of(i * ROWS, ROWS), ROWS), :].reshape(BLOCKS * ROWS, 2 * WIDTH)

        line, core = group // 2, group % 2
        if of_other:
            core = 1 - core
        if not back:
            return load, 2 * line + core
        return load, 2 * (line - back - core) + jnp.where(i == 0, core, 1 - core)

    return at


def own():
    return lax.axis_index("group"), lax.axis_index("peer")


def moved(value, source):
    count = lax.axis_size("group") * lax.axis_size("peer")
    pairs = [(source(t), t) for t in range(count) if source(t) >= 0]
    return lax.ppermute(value, AXES, pairs)


def across(value):
    return lax.all_to_all(value, "peer", 0, 0)


def swapped(value):
    return moved(value, lambda t: t ^ 4)


def shards(queries, keys_values, doc_lengths):
    chip = jnp.concatenate([keys_values, swapped(keys_values)], axis=0)
    pair_near = moved(chip, lambda t: t - 8 - 8 * (t // 4 % 2))
    own_mine = across(spread(keys_values))
    starts = row_starts(doc_lengths, own)
    near_mine = across(spread(pair_near))
    pair_far = moved(pair_near, lambda t: t - 16)
    own_other = swapped(own_mine)
    prepared = query_pairs(queries), starts

    def step(pieces, state, last=False):
        return attend(doc_lengths, prepared, pieces, state, last, own)

    state = step([(own_mine, tiles(False, 0)), (own_other, tiles(True, 0))], None)
    near_other = swapped(near_mine)
    far_mine = across(spread(pair_far))
    state = step([(near_mine, tiles(False, 1)), (near_other, tiles(True, 1))], state)
    far_other = swapped(far_mine)
    state = step([(far_mine, tiles(False, 3))], state)
    attended, log_total = step([(far_other, tiles(True, 3))], state, True)
    return attended, log_total.T


def solution(mesh):
    placed = (P(AXES, None), P(AXES, None), P())
    return jax.shard_map(shards, mesh=mesh, in_specs=placed, out_specs=(P(AXES, None), P(AXES, None)), check_vma=False)
```

```python
import functools
import math

import jax
import jax.numpy as jnp
from jax import lax
from jax.experimental import pallas as pl
from jax.experimental.pallas import tpu as pltpu
from jax.sharding import PartitionSpec as P


ROWS = 128
HEADS = 8
WIDTH = 128
BLOCKS = 4
CHUNK = 256
NEG = -1e30
LIMIT = 2.0**40
SCALE = math.log2(math.e) / math.sqrt(WIDTH)
F32 = jnp.float32
BF16 = jnp.bfloat16


def starts_at(doc_ref, pos):
    def step(d, carry):
        end, start = carry
        end = end + doc_ref[d]
        return end, jnp.where(end <= pos, end, start)

    return lax.fori_loop(0, doc_ref.shape[0], step, (jnp.int32(0), jnp.zeros_like(pos)), unroll=True)[1]


def starts_body(own, doc_ref, row_start):
    group, peer = own()
    row_pos = (group * 4 + peer) * ROWS + lax.broadcasted_iota(jnp.int32, (8, ROWS), 1)
    row_start[...] = starts_at(doc_ref, row_pos)


def row_starts(doc_lengths, own):
    return pl.pallas_call(
        functools.partial(starts_body, own),
        out_shape=pltpu.VMEM((8, ROWS), jnp.int32),
        in_specs=[pl.BlockSpec(memory_space=pltpu.SMEM)],
        out_specs=pl.BlockSpec(memory_space=pltpu.VMEM),
        compiler_params=pltpu.CompilerParams(vmem_limit_bytes=4 << 20),
    )(doc_lengths)


def pairs_body(q_ref, query):
    for h in range(HEADS):
        rows = slice(h // 2 * WIDTH, (h // 2 + 1) * WIDTH)
        query[rows, h % 2 * ROWS : (h % 2 + 1) * ROWS] = q_ref[:, h * WIDTH : (h + 1) * WIDTH].T


def query_pairs(queries):
    vmem = pl.BlockSpec(memory_space=pltpu.VMEM)
    return pl.pallas_call(
        pairs_body,
        out_shape=pltpu.VMEM((HEADS // 2 * WIDTH, 2 * ROWS), BF16),
        in_specs=[vmem],
        out_specs=vmem,
        compiler_params=pltpu.CompilerParams(vmem_limit_bytes=4 << 20),
    )(queries)


def spread_body(*refs):
    out, at = refs[-1], 0
    for ref in refs[:-1]:
        value = ref[...]
        for n in range(BLOCKS):
            out[n, at : at + value.shape[0]] = value
        at += value.shape[0]


def spread(*values):
    vmem = pl.BlockSpec(memory_space=pltpu.VMEM)
    rows = sum(v.shape[0] for v in values)
    return pl.pallas_call(
        spread_body,
        out_shape=pltpu.VMEM((BLOCKS, rows, 2 * WIDTH), BF16),
        in_specs=[vmem] * len(values),
        out_specs=vmem,
        compiler_params=pltpu.CompilerParams(vmem_limit_bytes=4 << 20),
    )(*(pltpu.with_memory_space_constraint(v, pltpu.VMEM) for v in values))


def attend_body(first, last, places, own, doc_ref, query, start_ref, *refs):
    kv_refs, refs = refs[: len(places)], refs[len(places) :]
    if not first:
        stat_in, acc_in, refs = refs[0], refs[1], refs[2:]
    if last:
        out, log_out, stat, acc, bias = refs
    else:
        stat, acc, bias = refs
    group, peer = own()
    q_first = (group * 4 + peer) * ROWS

    start_low = starts_at(doc_ref, q_first)
    start_high = starts_at(doc_ref, q_first + ROWS - 1)
    row_pos = q_first + lax.broadcasted_iota(jnp.int32, (1, ROWS), 1)
    row_start = start_ref[:1]
    span = BLOCKS * ROWS

    def pair_rows(values, h):
        return jnp.concatenate([values[h : h + 1], values[h + 1 : h + 2]], axis=1)

    def operands(tile):
        values = jnp.concatenate([tile[:, WIDTH:].T, jnp.ones((16, span), BF16)], axis=0)
        return tile[:, :WIDTH], values

    def set_bias(base, order):
        for n, place in enumerate(order):
            if not isinstance(order, range):
                place = (peer + place) % BLOCKS
            key_pos = base + place * ROWS + lax.broadcasted_iota(jnp.int32, (ROWS, ROWS), 0)
            hidden = jnp.where((key_pos >= row_start) & (key_pos <= row_pos), F32(0), F32(NEG))
            bias[n * ROWS : (n + 1) * ROWS, :ROWS] = hidden
            bias[n * ROWS : (n + 1) * ROWS, ROWS:] = hidden

    def exact(tile, base, order):
        keys, values = operands(tile)
        set_bias(base, order)

        for p in range(HEADS // 2):
            h = 2 * p
            score = jnp.dot(keys, query[p * WIDTH : (p + 1) * WIDTH], preferred_element_type=F32) * F32(SCALE) + bias[...]
            old = pair_rows(stat, h)
            new = jnp.maximum(old, jnp.max(score, axis=0, keepdims=True))
            fade = jnp.exp2(old - new)
            part = jnp.dot(values, jnp.exp2(score - new).astype(BF16), preferred_element_type=F32)
            for k in range(2):
                rows, cols = slice((h + k) * WIDTH, (h + k + 1) * WIDTH), slice(k * ROWS, (k + 1) * ROWS)
                acc[rows] = acc[rows] * fade[:, cols] + part[:WIDTH, cols]
                at = HEADS + h + k
                stat[at : at + 1] = stat[at : at + 1] * fade[:, cols] + part[WIDTH : WIDTH + 1, cols]
                stat[h + k : h + k + 1] = new[:, cols]

    def quick(tile, base, order, masked):
        keys, values = operands(tile)
        if masked:
            set_bias(base, order)
        steps = [(p, c) for p in range(HEADS // 2) for c in range(0, span, CHUNK)]

        def scores(step):
            p, c = step
            return jnp.dot(keys[c : c + CHUNK], query[p * WIDTH : (p + 1) * WIDTH], preferred_element_type=F32)

        ahead = scores(steps[0])
        part = None
        for n, (p, c) in enumerate(steps):
            h = 2 * p
            score = ahead
            if n + 1 < len(steps):
                ahead = scores(steps[n + 1])
            score = score * F32(SCALE) - pair_rows(stat, h)
            if masked:
                score = score + bias[c : c + CHUNK]
            weight = jnp.exp2(score).astype(BF16)
            piece = jnp.dot(values[:, c : c + CHUNK], weight, preferred_element_type=F32)
            part = piece if c == 0 else part + piece
            if c + CHUNK < span:
                continue
            for k in range(2):
                rows, cols = slice((h + k) * WIDTH, (h + k + 1) * WIDTH), slice(k * ROWS, (k + 1) * ROWS)
                acc[rows] += part[:WIDTH, cols]
                at = HEADS + h + k
                stat[at : at + 1] += part[WIDTH : WIDTH + 1, cols]

    def run(fast):
        if first:
            stat[:HEADS] = jnp.full((HEADS, ROWS), NEG, F32)
            stat[HEADS:] = jnp.zeros((HEADS, ROWS), F32)
            acc[...] = jnp.zeros_like(acc)
            if fast:
                own_keys = kv_refs[0][peer, :ROWS, :WIDTH].T.astype(F32)
                for h in range(HEADS):
                    rows, cols = slice(h // 2 * WIDTH, (h // 2 + 1) * WIDTH), slice(h % 2 * ROWS, (h % 2 + 1) * ROWS)
                    product = query[rows, cols].astype(F32) * own_keys
                    stat[h : h + 1] = jnp.sum(product, axis=0, keepdims=True) * F32(SCALE)
        else:
            stat[...] = stat_in[...]
            acc[...] = acc_in[...]

        for kv_ref, (slots, place) in zip(kv_refs, places):

            def body(i, _, kv_ref=kv_ref, place=place):
                load, tile_group, order = place(kv_ref, i, group)
                base = tile_group * span
                needed = (base + span > start_low) & (base < q_first + ROWS) & (base >= 0)
                whole = (base >= start_high) & (base + span <= q_first)
                if not fast:

                    @pl.when(needed)
                    def _():
                        exact(load(), base, order)

                    return 0

                @pl.when(needed & whole)
                def _():
                    quick(load(), base, order, False)

                @pl.when(needed & jnp.logical_not(whole))
                def _():
                    quick(load(), base, order, True)

                return 0

            lax.fori_loop(0, slots, body, 0)

    run(True)

    @pl.when(jnp.logical_not(jnp.max(stat[HEADS:]) <= F32(LIMIT)))
    def _():
        run(False)

    if last:
        stats = stat[...]
        inverse = 1.0 / stats[HEADS:]
        for h in range(HEADS):
            rows = slice(h * WIDTH, (h + 1) * WIDTH)
            out[:, rows] = (acc[rows] * inverse[h : h + 1]).T.astype(BF16)
        log_out[...] = stats[:HEADS] * F32(math.log(2.0)) + jnp.log(stats[HEADS:])


def attend(doc_lengths, prepared, pieces, state, last, own):
    places = [(kv.shape[1] // ROWS, place) for kv, place in pieces]
    vmem = pl.BlockSpec(memory_space=pltpu.VMEM)
    arrays = (*prepared, *(kv for kv, _ in pieces), *(state or ()))
    operands = [doc_lengths, *(pltpu.with_memory_space_constraint(a, pltpu.VMEM) for a in arrays)]
    state_shape = [(2 * HEADS, ROWS), (HEADS * WIDTH, ROWS)]
    bias = pltpu.VMEM((BLOCKS * ROWS, 2 * ROWS), F32)
    if last:
        out_shape = (
            jax.ShapeDtypeStruct((ROWS, HEADS * WIDTH), BF16),
            jax.ShapeDtypeStruct((HEADS, ROWS), F32),
        )
        scratch = [pltpu.VMEM(s, F32) for s in state_shape] + [bias]
    else:
        out_shape = tuple(pltpu.VMEM(s, F32) for s in state_shape)
        scratch = [bias]
    return pl.pallas_call(
        functools.partial(attend_body, state is None, last, places, own),
        out_shape=out_shape,
        in_specs=[pl.BlockSpec(memory_space=pltpu.SMEM)] + [vmem] * (len(operands) - 1),
        out_specs=(vmem, vmem),
        scratch_shapes=scratch,
        compiler_params=pltpu.CompilerParams(vmem_limit_bytes=16 << 20),
    )(*operands)


AXES = ("group", "peer")
TURNS = (0, 1, 3, 2)


def tiles(of_other, groups, turned=False):
    def at(kv_ref, i, group):
        def load():
            return kv_ref[:, pl.ds(pl.multiple_of(i * ROWS, ROWS), ROWS), :].reshape(BLOCKS * ROWS, 2 * WIDTH)

        line, core = group // 2, group % 2
        return load, groups(i, line, 1 - core if of_other else core), TURNS if turned else range(BLOCKS)

    return at


def near(i, line, core):
    pair = 2 * (line - 1 - core) + jnp.where(i == 1, core, 1 - core)
    return jnp.where(i == 0, 2 * line + core, pair)


def far(i, line, core):
    return 2 * (line - 3 - core) + jnp.where(i == 0, core, 1 - core)


def own():
    return lax.axis_index("group"), lax.axis_index("peer")


def moved(value, source):
    count = lax.axis_size("group") * lax.axis_size("peer")
    pairs = [(source(t), t) for t in range(count) if source(t) >= 0]
    return lax.ppermute(value, AXES, pairs)


def shards(queries, keys_values, doc_lengths):
    chip = jnp.concatenate([keys_values, moved(keys_values, lambda t: t ^ 4)], axis=0)
    pair_near = moved(chip, lambda t: t - 8 - 8 * (t // 4 % 2))
    pair_far = moved(chip, lambda t: t - 24 - 8 * (t // 4 % 2))
    starts = row_starts(doc_lengths, own)
    prepared = query_pairs(queries), starts
    near_mine = lax.all_to_all(spread(keys_values, pair_near), "peer", 0, 0)
    turns = []
    for k in (1, 3, 2):
        turns.append(moved(pair_far, lambda t, k=k: t // 4 * 4 + (t + k) % 4))
    far_mine = jnp.concatenate([pair_far, *turns], axis=0).reshape(BLOCKS, *pair_far.shape)
    near_other = moved(near_mine, lambda t: t ^ 4)
    far_other = moved(far_mine, lambda t: t ^ 4)
    pieces = [(near_mine, tiles(False, near)), (near_other, tiles(True, near)), (far_mine, tiles(False, far, True))]
    state = attend(doc_lengths, prepared, pieces, None, False, own)
    attended, log_total = attend(doc_lengths, prepared, [(far_other, tiles(True, far, True))], state, True, own)
    return attended, log_total.T


def solution(mesh):
    placed = (P(AXES, None), P(AXES, None), P())
    return jax.shard_map(shards, mesh=mesh, in_specs=placed, out_specs=(P(AXES, None), P(AXES, None)), check_vma=False)
```

```python
import functools
import math

import jax
import jax.numpy as jnp
from jax import lax
from jax.experimental import pallas as pl
from jax.experimental.pallas import tpu as pltpu
from jax.sharding import PartitionSpec as P


ROWS = 128
HEADS = 8
WIDTH = 128
BLOCKS = 4
CHUNK = 256
NEG = -1e30
LIMIT = 2.0**40
SCALE = math.log2(math.e) / math.sqrt(WIDTH)
F32 = jnp.float32
BF16 = jnp.bfloat16


def starts_at(doc_ref, pos):
    def step(d, carry):
        end, start = carry
        end = end + doc_ref[d]
        return end, jnp.where(end <= pos, end, start)

    return lax.fori_loop(0, doc_ref.shape[0], step, (jnp.int32(0), jnp.zeros_like(pos)), unroll=True)[1]


def starts_body(own, doc_ref, row_start):
    group, peer = own()
    row_pos = (group * 4 + peer) * ROWS + lax.broadcasted_iota(jnp.int32, (8, ROWS), 1)
    row_start[...] = starts_at(doc_ref, row_pos)


def row_starts(doc_lengths, own):
    return pl.pallas_call(
        functools.partial(starts_body, own),
        out_shape=pltpu.VMEM((8, ROWS), jnp.int32),
        in_specs=[pl.BlockSpec(memory_space=pltpu.SMEM)],
        out_specs=pl.BlockSpec(memory_space=pltpu.VMEM),
        compiler_params=pltpu.CompilerParams(vmem_limit_bytes=4 << 20),
    )(doc_lengths)


def pairs_body(q_ref, query):
    for h in range(HEADS):
        rows = slice(h // 2 * WIDTH, (h // 2 + 1) * WIDTH)
        query[rows, h % 2 * ROWS : (h % 2 + 1) * ROWS] = q_ref[:, h * WIDTH : (h + 1) * WIDTH].T


def query_pairs(queries):
    vmem = pl.BlockSpec(memory_space=pltpu.VMEM)
    return pl.pallas_call(
        pairs_body,
        out_shape=pltpu.VMEM((HEADS // 2 * WIDTH, 2 * ROWS), BF16),
        in_specs=[vmem],
        out_specs=vmem,
        compiler_params=pltpu.CompilerParams(vmem_limit_bytes=4 << 20),
    )(queries)


def spread_body(*refs):
    out, at = refs[-1], 0
    for ref in refs[:-1]:
        value = ref[...]
        for n in range(BLOCKS):
            out[n, at : at + value.shape[0]] = value
        at += value.shape[0]


def spread(*values):
    vmem = pl.BlockSpec(memory_space=pltpu.VMEM)
    rows = sum(v.shape[0] for v in values)
    return pl.pallas_call(
        spread_body,
        out_shape=pltpu.VMEM((BLOCKS, rows, 2 * WIDTH), BF16),
        in_specs=[vmem] * len(values),
        out_specs=vmem,
        compiler_params=pltpu.CompilerParams(vmem_limit_bytes=4 << 20),
    )(*(pltpu.with_memory_space_constraint(v, pltpu.VMEM) for v in values))


def attend_body(first, last, places, own, doc_ref, query, start_ref, *refs):
    kv_refs, refs = refs[: len(places)], refs[len(places) :]
    if not first:
        stat_in, acc_in, refs = refs[0], refs[1], refs[2:]
    if last:
        out, log_out, stat, acc, bias = refs
    else:
        stat, acc, bias = refs
    group, peer = own()
    q_first = (group * 4 + peer) * ROWS

    start_low = starts_at(doc_ref, q_first)
    start_high = starts_at(doc_ref, q_first + ROWS - 1)
    row_pos = q_first + lax.broadcasted_iota(jnp.int32, (1, ROWS), 1)
    row_start = start_ref[:1]
    span = BLOCKS * ROWS

    def pair_rows(values, h):
        return jnp.concatenate([values[h : h + 1], values[h + 1 : h + 2]], axis=1)

    def operands(tile):
        values = jnp.concatenate([tile[:, WIDTH:].T, jnp.ones((16, span), BF16)], axis=0)
        return tile[:, :WIDTH], values

    def set_bias(base, order):
        for n, place in enumerate(order):
            if not isinstance(order, range):
                place = (peer + place) % BLOCKS
            key_pos = base + place * ROWS + lax.broadcasted_iota(jnp.int32, (ROWS, ROWS), 0)
            hidden = jnp.where((key_pos >= row_start) & (key_pos <= row_pos), F32(0), F32(NEG))
            bias[n * ROWS : (n + 1) * ROWS, :ROWS] = hidden
            bias[n * ROWS : (n + 1) * ROWS, ROWS:] = hidden

    def exact(tile, base, order):
        keys, values = operands(tile)
        set_bias(base, order)

        for p in range(HEADS // 2):
            h = 2 * p
            score = jnp.dot(keys, query[p * WIDTH : (p + 1) * WIDTH], preferred_element_type=F32) * F32(SCALE) + bias[...]
            old = pair_rows(stat, h)
            new = jnp.maximum(old, jnp.max(score, axis=0, keepdims=True))
            fade = jnp.exp2(old - new)
            part = jnp.dot(values, jnp.exp2(score - new).astype(BF16), preferred_element_type=F32)
            for k in range(2):
                rows, cols = slice((h + k) * WIDTH, (h + k + 1) * WIDTH), slice(k * ROWS, (k + 1) * ROWS)
                acc[rows] = acc[rows] * fade[:, cols] + part[:WIDTH, cols]
                at = HEADS + h + k
                stat[at : at + 1] = stat[at : at + 1] * fade[:, cols] + part[WIDTH : WIDTH + 1, cols]
                stat[h + k : h + k + 1] = new[:, cols]

    def quick(tile, base, order, masked):
        keys, values = operands(tile)
        if masked:
            set_bias(base, order)
        steps = [(p, c) for p in range(HEADS // 2) for c in range(0, span, CHUNK)]

        def scores(step):
            p, c = step
            return jnp.dot(keys[c : c + CHUNK], query[p * WIDTH : (p + 1) * WIDTH], preferred_element_type=F32)

        ahead = scores(steps[0])
        part = None
        for n, (p, c) in enumerate(steps):
            h = 2 * p
            score = ahead
            if n + 1 < len(steps):
                ahead = scores(steps[n + 1])
            score = score * F32(SCALE) - pair_rows(stat, h)
            if masked:
                score = score + bias[c : c + CHUNK]
            weight = jnp.exp2(score).astype(BF16)
            piece = jnp.dot(values[:, c : c + CHUNK], weight, preferred_element_type=F32)
            part = piece if c == 0 else part + piece
            if c + CHUNK < span:
                continue
            for k in range(2):
                rows, cols = slice((h + k) * WIDTH, (h + k + 1) * WIDTH), slice(k * ROWS, (k + 1) * ROWS)
                acc[rows] += part[:WIDTH, cols]
                at = HEADS + h + k
                stat[at : at + 1] += part[WIDTH : WIDTH + 1, cols]

    def run(fast):
        if first:
            stat[:HEADS] = jnp.full((HEADS, ROWS), NEG, F32)
            stat[HEADS:] = jnp.zeros((HEADS, ROWS), F32)
            acc[...] = jnp.zeros_like(acc)
            if fast:
                own_keys = kv_refs[0][peer, :ROWS, :WIDTH].T.astype(F32)
                for h in range(HEADS):
                    rows, cols = slice(h // 2 * WIDTH, (h // 2 + 1) * WIDTH), slice(h % 2 * ROWS, (h % 2 + 1) * ROWS)
                    product = query[rows, cols].astype(F32) * own_keys
                    stat[h : h + 1] = jnp.sum(product, axis=0, keepdims=True) * F32(SCALE)
        else:
            stat[...] = stat_in[...]
            acc[...] = acc_in[...]

        for kv_ref, (slots, place) in zip(kv_refs, places):

            def body(i, _, kv_ref=kv_ref, place=place):
                load, tile_group, order = place(kv_ref, i, group)
                base = tile_group * span
                needed = (base + span > start_low) & (base < q_first + ROWS) & (base >= 0)
                whole = (base >= start_high) & (base + span <= q_first)
                if not fast:

                    @pl.when(needed)
                    def _():
                        exact(load(), base, order)

                    return 0

                @pl.when(needed & whole)
                def _():
                    quick(load(), base, order, False)

                @pl.when(needed & jnp.logical_not(whole))
                def _():
                    quick(load(), base, order, True)

                return 0

            lax.fori_loop(0, slots, body, 0)

    run(True)

    @pl.when(jnp.logical_not(jnp.max(stat[HEADS:]) <= F32(LIMIT)))
    def _():
        run(False)

    if last:
        stats = stat[...]
        inverse = 1.0 / stats[HEADS:]
        for h in range(HEADS):
            rows = slice(h * WIDTH, (h + 1) * WIDTH)
            out[:, rows] = (acc[rows] * inverse[h : h + 1]).T.astype(BF16)
        log_out[...] = stats[:HEADS] * F32(math.log(2.0)) + jnp.log(stats[HEADS:])


def attend(doc_lengths, prepared, pieces, state, last, own):
    places = [(kv.shape[1] // ROWS, place) for kv, place in pieces]
    vmem = pl.BlockSpec(memory_space=pltpu.VMEM)
    arrays = (*prepared, *(kv for kv, _ in pieces), *(state or ()))
    operands = [doc_lengths, *(pltpu.with_memory_space_constraint(a, pltpu.VMEM) for a in arrays)]
    state_shape = [(2 * HEADS, ROWS), (HEADS * WIDTH, ROWS)]
    bias = pltpu.VMEM((BLOCKS * ROWS, 2 * ROWS), F32)
    if last:
        out_shape = (
            jax.ShapeDtypeStruct((ROWS, HEADS * WIDTH), BF16),
            jax.ShapeDtypeStruct((HEADS, ROWS), F32),
        )
        scratch = [pltpu.VMEM(s, F32) for s in state_shape] + [bias]
    else:
        out_shape = tuple(pltpu.VMEM(s, F32) for s in state_shape)
        scratch = [bias]
    return pl.pallas_call(
        functools.partial(attend_body, state is None, last, places, own),
        out_shape=out_shape,
        in_specs=[pl.BlockSpec(memory_space=pltpu.SMEM)] + [vmem] * (len(operands) - 1),
        out_specs=(vmem, vmem),
        scratch_shapes=scratch,
        compiler_params=pltpu.CompilerParams(vmem_limit_bytes=16 << 20),
    )(*operands)


AXES = ("group", "peer")
TURNS = (0, 1, 3, 2)


def tiles(of_other, groups, turned=False):
    def at(kv_ref, i, group):
        def load():
            return kv_ref[:, pl.ds(pl.multiple_of(i * ROWS, ROWS), ROWS), :].reshape(BLOCKS * ROWS, 2 * WIDTH)

        line, core = group // 2, group % 2
        return load, groups(i, line, 1 - core if of_other else core), TURNS if turned else range(BLOCKS)

    return at


def near(i, line, core):
    pair = 2 * (line - 1 - core) + jnp.where(i == 1, core, 1 - core)
    return jnp.where(i == 0, 2 * line + core, pair)


def far(i, line, core):
    return 2 * (line - 3 - core) + jnp.where(i == 0, core, 1 - core)


def own():
    return lax.axis_index("group"), lax.axis_index("peer")


def moved(value, source):
    count = lax.axis_size("group") * lax.axis_size("peer")
    pairs = [(source(t), t) for t in range(count) if source(t) >= 0]
    return lax.ppermute(value, AXES, pairs)


def shards(queries, keys_values, doc_lengths):
    chip = jnp.concatenate([keys_values, moved(keys_values, lambda t: t ^ 4)], axis=0)
    pair_near = moved(chip, lambda t: t - 8 - 8 * (t // 4 % 2))
    pair_far = moved(chip, lambda t: t - 24 - 8 * (t // 4 % 2))
    starts = row_starts(doc_lengths, own)
    prepared = query_pairs(queries), starts
    near_mine = lax.all_to_all(spread(keys_values, pair_near), "peer", 0, 0)
    turns = []
    for k in (1, 3, 2):
        turns.append(moved(pair_far, lambda t, k=k: t // 4 * 4 + (t + k) % 4))
    far_mine = jnp.concatenate([pair_far, *turns], axis=0).reshape(BLOCKS, *pair_far.shape)
    near_other = moved(near_mine, lambda t: t ^ 4)
    far_other = moved(far_mine, lambda t: t ^ 4)
    state = attend(doc_lengths, prepared, [(near_mine, tiles(False, near))], None, False, own)
    pieces = [(near_other, tiles(True, near)), (far_mine, tiles(False, far, True))]
    state = attend(doc_lengths, prepared, pieces, state, False, own)
    attended, log_total = attend(doc_lengths, prepared, [(far_other, tiles(True, far, True))], state, True, own)
    return attended, log_total.T


def solution(mesh):
    placed = (P(AXES, None), P(AXES, None), P())
    return jax.shard_map(shards, mesh=mesh, in_specs=placed, out_specs=(P(AXES, None), P(AXES, None)), check_vma=False)
```
